512 devices in a mesh: bl: 32 (over y, x, core), dir: 16 (over z).
Axes of the slice: x: 4, y: 4, z: 16, core: 2. Of those that a mesh axis runs over, the one named last changes fastest.
Arguments:
- visibilities: float32 [8, 16, 8192], P(None, 'dir', 'bl'), may hold values from -24 to 24
- coherencies: bfloat16 [32, 8, 16, 8192], P('dir', None, None, 'bl'), may hold values from -6 to 6
- gain_offsets: float32 [32, 8, 512], P(None, None, 'bl'), may hold values from -1.5 to 1.5
- stations: int32 [2, 8192], P(None, 'bl'), may hold values from 0 to 511, as said below
- solve_order: int32 [32], replicated, may hold values from 0 to 31, each once
- counts: int32 [32], replicated, may hold values from 1 to 2
- damping: int32 [32], replicated, may hold values from 1 to 8
Outputs:
- gains: float32 [32, 8, 512], P(None, None, 'bl')
- residual: float32 [8, 16, 8192], P(None, 'dir', 'bl')
The draws below stay inside these ranges and needn't reach their ends.
Inputs may be any that keep to these rules, and one draw needn't show every extreme that they name: Each baseline names two different stations. `solve_order`: each direction appears once.
All inputs are finite; a program needn't handle non-finite values.
Results may differ from the reference program's by a relative error of at most 0.0003.
Values may be sent and summed in bfloat16 or wider, within the bound.
A program may use at most 64 MiB of HBM per device.

```python
import jax
import jax.numpy as jnp
from jax import lax

STATION_TOTAL = 512
DIRECTION_COUNT = 32
FREQUENCY_COUNT = 16
LM_ITERS = 2
SOLVED = 4
BASELINE_TOTAL = 8192


def draw_stations(key, part):
    leading_random_key = jax.random.fold_in(key, 11)
    trailing_random_key = jax.random.fold_in(key, 12)
    leading_endpoint = jax.random.randint(leading_random_key, (BASELINE_TOTAL,), 0, STATION_TOTAL)
    gain_shifts = jax.random.randint(trailing_random_key, (BASELINE_TOTAL,), 1, STATION_TOTAL)
    return jnp.stack([leading_endpoint, (leading_endpoint + gain_shifts) % STATION_TOTAL]).astype(jnp.int32)


def draw_counts(key, part):
    chosen = jax.random.randint(jax.random.fold_in(key, 21), (DIRECTION_COUNT,), 1, LM_ITERS + 1)
    position = jax.random.randint(jax.random.fold_in(key, 22), (), 0, DIRECTION_COUNT)
    return jnp.where(jnp.arange(DIRECTION_COUNT) == position, LM_ITERS, chosen).astype(jnp.int32)


def touch_ends(values, own_key, least, high):
    spot = [jax.random.randint(jax.random.fold_in(own_key, axis), (), 0, length) for axis, length in enumerate(values.shape)]
    main_axis = values.shape.index(max(values.shape))
    neighbour = spot[:main_axis] + [(spot[main_axis] + 1) % values.shape[main_axis]] + spot[main_axis + 1:]
    return values.at[tuple(spot)].set(least).at[tuple(neighbour)].set(high)


def block_scale(rng, dims, cuts, least, top_value):
    def one(axis_at, shards_of):
        heights = jax.random.uniform(jax.random.fold_in(jax.random.fold_in(rng, 6), axis_at), (shards_of,), jnp.float32, least / len(cuts), top_value / len(cuts))
        return jnp.repeat(jnp.exp(heights), dims[axis_at] // shards_of).reshape((-1,) + (1,) * (len(dims) - axis_at - 1))

    loudness = one(*cuts[0])
    for cut in cuts[1:]:
        loudness = loudness * one(*cut)
    return loudness


def bell_draw(stream_key, dims, deviation, limit, cuts=(), dtype=jnp.bfloat16):
    array = deviation * jax.random.normal(stream_key, dims, jnp.float32)
    if cuts:
        array = array * block_scale(stream_key, dims, cuts, -0.22, 0.18)
    return jnp.clip(array, -limit, limit).astype(dtype)


def setup_inputs(seed: int = 0) -> dict:
    keys = jax.random.split(jax.random.key(seed), 8)
    return {
        "visibilities": bell_draw(keys[0], (8, FREQUENCY_COUNT, BASELINE_TOTAL), 4.0, 24.0, ((1, 16), (2, 32)), jnp.float32),
        "coherencies": bell_draw(keys[1], (DIRECTION_COUNT, 8, FREQUENCY_COUNT, BASELINE_TOTAL), 1.0, 6.0, ((0, 16), (3, 32))),
        "gain_offsets": bell_draw(keys[2], (DIRECTION_COUNT, 8, STATION_TOTAL), 0.3, 1.5, ((2, 32),), jnp.float32),
        "stations": draw_stations(jax.random.fold_in(keys[7], 71), 0),
        "solve_order": jax.random.permutation(keys[4], DIRECTION_COUNT).astype(jnp.int32),
        "counts": draw_counts(jax.random.fold_in(keys[7], 71), 0),
        "damping": touch_ends(jax.random.randint(keys[6], (DIRECTION_COUNT,), 1, 9), jax.random.fold_in(keys[6], 1), 1, 8).astype(jnp.int32),
    }


def matrix_entry(mat, i, j):
    return mat[4 * i + 2 * j], mat[4 * i + 2 * j + 1]


def matmul_two(left, right):
    pieces = []
    for i in (0, 1):
        for j in (0, 1):
            left_r0, left_i0 = matrix_entry(left, i, 0)
            left_r1, left_i1 = matrix_entry(left, i, 1)
            right_r0, right_i0 = matrix_entry(right, 0, j)
            right_r1, right_i1 = matrix_entry(right, 1, j)
            pieces.append(left_r0 * right_r0 - left_i0 * right_i0 + left_r1 * right_r1 - left_i1 * right_i1)
            pieces.append(left_r0 * right_i0 + left_i0 * right_r0 + left_r1 * right_i1 + left_i1 * right_r1)
    return jnp.stack(pieces)


def adjoint(mat):
    return jnp.stack([mat[0], -mat[1], mat[4], -mat[5], mat[2], -mat[3], mat[6], -mat[7]])


def apply_gains(gain_p, coher_now, gain_q):
    return matmul_two(matmul_two(gain_p, coher_now), adjoint(gain_q))


def gram_parts(gram):
    return jnp.stack([gram[0], gram[6], gram[2], gram[3]])


def station_terms(gain_p, gain_q, coher_now, target):
    z_rows = matmul_two(coher_now, adjoint(gain_q))
    y_rows = matmul_two(adjoint(coher_now), adjoint(gain_p))
    leading_endpoint = jnp.concatenate([matmul_two(target, adjoint(z_rows)), gram_parts(matmul_two(z_rows, adjoint(z_rows)))], 0)
    second = jnp.concatenate([matmul_two(adjoint(target), adjoint(y_rows)), gram_parts(matmul_two(y_rows, adjoint(y_rows)))], 0)
    return jnp.sum(leading_endpoint, axis=1), jnp.sum(second, axis=1)


def to_stations(leading_endpoint, second, stations, count):
    totals = jax.ops.segment_sum(leading_endpoint.T, stations[0], count) + jax.ops.segment_sum(second.T, stations[1], count)
    return totals.T


def solve_station(gathered_sums, gain_now, damp_value):
    numerator = gathered_sums[:8] + damp_value * gain_now
    diag_a = gathered_sums[8] + damp_value
    diag_d = gathered_sums[9] + damp_value
    cross_r = gathered_sums[10]
    cross_i = gathered_sums[11]
    determinant = diag_a * diag_d - cross_r * cross_r - cross_i * cross_i
    zeros_row = jnp.zeros_like(determinant)
    inverse = jnp.stack([diag_d, zeros_row, -cross_r, -cross_i, -cross_r, cross_i, diag_a, zeros_row]) / determinant
    return matmul_two(numerator, inverse)


def reference(visibilities, coherencies, gain_offsets, stations, solve_order, counts, damping):
    identity = jnp.zeros((8,), jnp.float32).at[0].set(1.0).at[6].set(1.0)
    start = gain_offsets + identity[None, :, None]
    damping_factor = BASELINE_TOTAL * FREQUENCY_COUNT / STATION_TOTAL

    def direction_model(gain_now, coher_now):
        gain_p = jnp.take(gain_now, stations[0], axis=1)[:, None, :]
        gain_q = jnp.take(gain_now, stations[1], axis=1)[:, None, :]
        return apply_gains(gain_p, coher_now, gain_q)

    def add_model(which, acc):
        return acc + direction_model(start[which], coherencies[which].astype(jnp.float32))

    first_model = lax.fori_loop(0, DIRECTION_COUNT, add_model, jnp.zeros(visibilities.shape, jnp.float32))
    first_residual = visibilities - first_model

    def sweep(step_index, state):
        gain_table, residual = state
        which = solve_order[step_index]
        coher_now = coherencies[which].astype(jnp.float32)
        damp_value = damping[which].astype(jnp.float32) * damping_factor
        gain_start = gain_table[which]
        target = residual + direction_model(gain_start, coher_now)

        def iterate(round_index, gain_now):
            gain_p = jnp.take(gain_now, stations[0], axis=1)[:, None, :]
            gain_q = jnp.take(gain_now, stations[1], axis=1)[:, None, :]
            leading_endpoint, second = station_terms(gain_p, gain_q, coher_now, target)
            gathered_sums = to_stations(leading_endpoint, second, stations, STATION_TOTAL)
            updated = solve_station(gathered_sums, gain_now, damp_value)
            return jnp.where(round_index < counts[which], updated, gain_now)

        gain_final = lax.fori_loop(0, LM_ITERS, iterate, gain_start)
        residual = target - direction_model(gain_final, coher_now)
        return gain_table.at[which].set(gain_final), residual

    gains, residual = lax.fori_loop(0, SOLVED, sweep, (start, first_residual))
    return gains, residual
```

```python
import jax
import jax.numpy as jnp
from jax import lax
from jax.sharding import PartitionSpec as P

LM_ITERS = 2
SOLVED = 4


def matrix_entry(mat, i, j):
    return (mat[4 * i + 2 * j], mat[4 * i + 2 * j + 1])


def matmul_two(left, right):
    pieces = []
    for i in (0, 1):
        for j in (0, 1):
            left_r0, left_i0 = matrix_entry(left, i, 0)
            left_r1, left_i1 = matrix_entry(left, i, 1)
            right_r0, right_i0 = matrix_entry(right, 0, j)
            right_r1, right_i1 = matrix_entry(right, 1, j)
            pieces.append(
                left_r0 * right_r0 - left_i0 * right_i0 + left_r1 * right_r1 - left_i1 * right_i1
            )
            pieces.append(
                left_r0 * right_i0 + left_i0 * right_r0 + left_r1 * right_i1 + left_i1 * right_r1
            )
    return jnp.stack(pieces)


def adjoint(mat):
    return jnp.stack([mat[0], -mat[1], mat[4], -mat[5], mat[2], -mat[3], mat[6], -mat[7]])


def apply_gains(gain_p, coher_now, gain_q):
    return matmul_two(matmul_two(gain_p, coher_now), adjoint(gain_q))


def gram_parts(gram):
    return jnp.stack([gram[0], gram[6], gram[2], gram[3]])


def station_terms(gain_p, gain_q, coher_now, target):
    z_rows = matmul_two(coher_now, adjoint(gain_q))
    y_rows = matmul_two(adjoint(coher_now), adjoint(gain_p))
    leading_endpoint = jnp.concatenate(
        [matmul_two(target, adjoint(z_rows)), gram_parts(matmul_two(z_rows, adjoint(z_rows)))], 0
    )
    second = jnp.concatenate(
        [
            matmul_two(adjoint(target), adjoint(y_rows)),
            gram_parts(matmul_two(y_rows, adjoint(y_rows))),
        ],
        0,
    )
    return (jnp.sum(leading_endpoint, axis=1), jnp.sum(second, axis=1))


def solve_station(gathered_sums, gain_now, damp_value):
    numerator = gathered_sums[:8] + damp_value * gain_now
    diag_a = gathered_sums[8] + damp_value
    diag_d = gathered_sums[9] + damp_value
    cross_r = gathered_sums[10]
    cross_i = gathered_sums[11]
    determinant = diag_a * diag_d - cross_r * cross_r - cross_i * cross_i
    zeros_row = jnp.zeros_like(determinant)
    inverse = (
        jnp.stack([diag_d, zeros_row, -cross_r, -cross_i, -cross_r, cross_i, diag_a, zeros_row])
        / determinant
    )
    return matmul_two(numerator, inverse)


def on_device(visibilities, coherencies, gain_offsets, stations, solve_order, counts, damping):
    identity = jnp.zeros((8,), jnp.float32).at[0].set(1.0).at[6].set(1.0)
    start = lax.all_gather(gain_offsets, "bl", axis=2, tiled=True) + identity[None, :, None]
    groups = lax.axis_size("bl")
    total_channels = coherencies.shape[2]
    station_count = start.shape[2]
    damping_factor = visibilities.shape[2] * groups * total_channels / station_count
    coher_all = lax.all_to_all(coherencies, "dir", 2, 0, tiled=True)
    ends_p = jnp.take(start, stations[0], axis=2)
    ends_q = jnp.take(start, stations[1], axis=2)
    gain_p = jnp.transpose(ends_p, (1, 0, 2))[:, :, None, :]
    gain_q = jnp.transpose(ends_q, (1, 0, 2))[:, :, None, :]
    coher_f32 = jnp.transpose(coher_all, (1, 0, 2, 3)).astype(jnp.float32)
    first_model = jnp.sum(apply_gains(gain_p, coher_f32, gain_q), axis=1)
    first_residual = visibilities - first_model

    def direction_model(gain_now, coher_now):
        gain_p = jnp.take(gain_now, stations[0], axis=1)[:, None, :]
        gain_q = jnp.take(gain_now, stations[1], axis=1)[:, None, :]
        return apply_gains(gain_p, coher_now, gain_q)

    def sweep(step_index, state):
        gain_table, residual = state
        which = solve_order[step_index]
        coher_now = lax.dynamic_index_in_dim(coher_all, which, 0, keepdims=False).astype(
            jnp.float32
        )
        damp_value = damping[which].astype(jnp.float32) * damping_factor
        gain_start = gain_table[which]
        target = residual + direction_model(gain_start, coher_now)

        def iterate(round_index, gain_now):
            gain_p = jnp.take(gain_now, stations[0], axis=1)[:, None, :]
            gain_q = jnp.take(gain_now, stations[1], axis=1)[:, None, :]
            leading_endpoint, second = station_terms(gain_p, gain_q, coher_now, target)
            local_sums = (
                jax.ops.segment_sum(leading_endpoint.T, stations[0], station_count)
                + jax.ops.segment_sum(second.T, stations[1], station_count)
            ).T
            gathered_sums = lax.psum(local_sums, ("bl", "dir"))
            return solve_station(gathered_sums, gain_now, damp_value)

        rounds = jnp.clip(counts[which], 0, LM_ITERS)
        gain_final = lax.fori_loop(0, rounds, iterate, gain_start)
        residual = target - direction_model(gain_final, coher_now)
        return (gain_table.at[which].set(gain_final), residual)

    gain_table, residual = lax.fori_loop(0, SOLVED, sweep, (start, first_residual))
    own_width = station_count // groups
    gains = lax.dynamic_slice_in_dim(gain_table, lax.axis_index("bl") * own_width, own_width, 2)
    return (gains, residual)


def solution(mesh):
    return jax.shard_map(
        on_device,
        mesh=mesh,
        in_specs=(
            P(None, "dir", "bl"),
            P("dir", None, None, "bl"),
            P(None, None, "bl"),
            P(None, "bl"),
            P(),
            P(),
            P(),
        ),
        out_specs=(P(None, None, "bl"), P(None, "dir", "bl")),
        check_vma=False,
    )
```

```python
import functools

import jax
import jax.numpy as jnp
from jax import lax
from jax.sharding import PartitionSpec as P
from jax.experimental import pallas as pl
from jax.experimental.pallas import tpu as pltpu

MESH_ID = pl.DeviceIdType.MESH

LM_ITERS = 2
SOLVED = 4


def matrix_entry(mat, i, j):
    return (mat[4 * i + 2 * j], mat[4 * i + 2 * j + 1])


def matmul_two(left, right):
    pieces = []
    for i in (0, 1):
        for j in (0, 1):
            left_r0, left_i0 = matrix_entry(left, i, 0)
            left_r1, left_i1 = matrix_entry(left, i, 1)
            right_r0, right_i0 = matrix_entry(right, 0, j)
            right_r1, right_i1 = matrix_entry(right, 1, j)
            pieces.append(
                left_r0 * right_r0 - left_i0 * right_i0 + left_r1 * right_r1 - left_i1 * right_i1
            )
            pieces.append(
                left_r0 * right_i0 + left_i0 * right_r0 + left_r1 * right_i1 + left_i1 * right_r1
            )
    return jnp.stack(pieces)


def adjoint(mat):
    return jnp.stack([mat[0], -mat[1], mat[4], -mat[5], mat[2], -mat[3], mat[6], -mat[7]])


def apply_gains(gain_p, coher_now, gain_q):
    return matmul_two(matmul_two(gain_p, coher_now), adjoint(gain_q))


def gram_parts(gram):
    return jnp.stack([gram[0], gram[6], gram[2], gram[3]])


def station_terms(gain_p, gain_q, coher_now, target):
    z_rows = matmul_two(coher_now, adjoint(gain_q))
    y_rows = matmul_two(adjoint(coher_now), adjoint(gain_p))
    leading_endpoint = jnp.concatenate(
        [matmul_two(target, adjoint(z_rows)), gram_parts(matmul_two(z_rows, adjoint(z_rows)))], 0
    )
    second = jnp.concatenate(
        [
            matmul_two(adjoint(target), adjoint(y_rows)),
            gram_parts(matmul_two(y_rows, adjoint(y_rows))),
        ],
        0,
    )
    return (jnp.sum(leading_endpoint, axis=1), jnp.sum(second, axis=1))


def solve_station(gathered_sums, gain_now, damp_value):
    numerator = gathered_sums[:8] + damp_value * gain_now
    diag_a = gathered_sums[8] + damp_value
    diag_d = gathered_sums[9] + damp_value
    cross_r = gathered_sums[10]
    cross_i = gathered_sums[11]
    determinant = diag_a * diag_d - cross_r * cross_r - cross_i * cross_i
    zeros_row = jnp.zeros_like(determinant)
    inverse = (
        jnp.stack([diag_d, zeros_row, -cross_r, -cross_i, -cross_r, cross_i, diag_a, zeros_row])
        / determinant
    )
    return matmul_two(numerator, inverse)


def all_reduce_kernel(nz, nb, x_ref, o_ref, r1, r2, r3, s1, q1, s2, q2, s3, q3):
    mz = lax.axis_index("dir")
    mb = lax.axis_index("bl")
    z_peers = [lax.rem(mz + k, nz) for k in range(1, nz)]
    b_peers = [lax.rem(mb + k, nb) for k in range(1, nb)]

    barrier = pltpu.get_barrier_semaphore()
    for p in z_peers:
        pl.semaphore_signal(barrier, 1, device_id=(mb, p), device_id_type=MESH_ID)
    for p in b_peers:
        pl.semaphore_signal(barrier, 1, device_id=(p, mz), device_id_type=MESH_ID)
    pl.semaphore_wait(barrier, (nz - 1) + (nb - 1))

    def exchange(peers, src_of, buf, me, send_sems, recv_sems, device_of):
        sent = []
        for p in peers:
            c = pltpu.make_async_remote_copy(
                src_ref=src_of(p),
                dst_ref=buf.at[me],
                send_sem=send_sems.at[p],
                recv_sem=recv_sems.at[me],
                device_id=device_of(p),
                device_id_type=MESH_ID,
            )
            c.start()
            sent.append(c)
        for p in peers:
            pltpu.make_async_remote_copy(
                src_ref=buf.at[p],
                dst_ref=buf.at[p],
                send_sem=send_sems.at[p],
                recv_sem=recv_sems.at[p],
                device_id=device_of(p),
                device_id_type=MESH_ID,
            ).wait_recv()
        for c in sent:
            c.wait_send()

    exchange(z_peers, lambda p: x_ref.at[p], r1, mz, s1, q1, lambda p: (mb, p))
    own = x_ref[mz]
    for p in z_peers:
        own = own + r1[p]
    r2[mb] = own
    exchange(b_peers, lambda p: r2.at[mb], r2, mb, s2, q2, lambda p: (p, mz))
    total = r2[mb]
    for p in b_peers:
        total = total + r2[p]
    r3[mz] = total
    exchange(z_peers, lambda p: r3.at[mz], r3, mz, s3, q3, lambda p: (mb, p))
    o_ref[...] = r3[...]


def all_reduce(payload, nz, nb):
    chunk_shape = payload.shape[1:]
    return pl.pallas_call(
        functools.partial(all_reduce_kernel, nz, nb),
        out_shape=jax.ShapeDtypeStruct(payload.shape, payload.dtype),
        in_specs=[pl.BlockSpec(memory_space=pltpu.VMEM)],
        out_specs=pl.BlockSpec(memory_space=pltpu.VMEM),
        scratch_shapes=[
            pltpu.VMEM((nz,) + chunk_shape, payload.dtype),
            pltpu.VMEM((nb,) + chunk_shape, payload.dtype),
            pltpu.VMEM((nz,) + chunk_shape, payload.dtype),
            pltpu.SemaphoreType.DMA((nz,)),
            pltpu.SemaphoreType.DMA((nz,)),
            pltpu.SemaphoreType.DMA((nb,)),
            pltpu.SemaphoreType.DMA((nb,)),
            pltpu.SemaphoreType.DMA((nz,)),
            pltpu.SemaphoreType.DMA((nz,)),
        ],
        compiler_params=pltpu.CompilerParams(collective_id=0, has_side_effects=True),
    )(payload)


def station_sum(rows, nz, nb):
    flat = rows.reshape(nz, -1, 128)
    return all_reduce(flat, nz, nb).reshape(rows.shape)


def on_device(visibilities, coherencies, gain_offsets, stations, solve_order, counts, damping):
    identity = jnp.zeros((8,), jnp.float32).at[0].set(1.0).at[6].set(1.0)
    start = lax.all_gather(gain_offsets, "bl", axis=2, tiled=True) + identity[None, :, None]
    groups = lax.axis_size("bl")
    nz = lax.axis_size("dir")
    total_channels = coherencies.shape[2]
    station_count = start.shape[2]
    damping_factor = visibilities.shape[2] * groups * total_channels / station_count
    coher_all = lax.all_to_all(coherencies, "dir", 2, 0, tiled=True)
    ends_p = jnp.take(start, stations[0], axis=2)
    ends_q = jnp.take(start, stations[1], axis=2)
    gain_p = jnp.transpose(ends_p, (1, 0, 2))[:, :, None, :]
    gain_q = jnp.transpose(ends_q, (1, 0, 2))[:, :, None, :]
    coher_f32 = jnp.transpose(coher_all, (1, 0, 2, 3)).astype(jnp.float32)
    first_model = jnp.sum(apply_gains(gain_p, coher_f32, gain_q), axis=1)
    first_residual = visibilities - first_model

    def direction_model(gain_now, coher_now):
        gain_p = jnp.take(gain_now, stations[0], axis=1)[:, None, :]
        gain_q = jnp.take(gain_now, stations[1], axis=1)[:, None, :]
        return apply_gains(gain_p, coher_now, gain_q)

    def sweep(step_index, state):
        gain_table, residual = state
        which = solve_order[step_index]
        coher_now = lax.dynamic_index_in_dim(coher_all, which, 0, keepdims=False).astype(
            jnp.float32
        )
        damp_value = damping[which].astype(jnp.float32) * damping_factor
        gain_start = gain_table[which]
        target = residual + direction_model(gain_start, coher_now)

        def iterate(round_index, gain_now):
            gain_p = jnp.take(gain_now, stations[0], axis=1)[:, None, :]
            gain_q = jnp.take(gain_now, stations[1], axis=1)[:, None, :]
            leading_endpoint, second = station_terms(gain_p, gain_q, coher_now, target)
            local_rows = jax.ops.segment_sum(
                leading_endpoint.T, stations[0], station_count
            ) + jax.ops.segment_sum(second.T, stations[1], station_count)
            gathered_sums = station_sum(local_rows, nz, groups).T
            return solve_station(gathered_sums, gain_now, damp_value)

        rounds = jnp.clip(counts[which], 0, LM_ITERS)
        gain_final = lax.fori_loop(0, rounds, iterate, gain_start)
        residual = target - direction_model(gain_final, coher_now)
        return (gain_table.at[which].set(gain_final), residual)

    gain_table, residual = lax.fori_loop(0, SOLVED, sweep, (start, first_residual))
    own_width = station_count // groups
    gains = lax.dynamic_slice_in_dim(gain_table, lax.axis_index("bl") * own_width, own_width, 2)
    return (gains, residual)


def solution(mesh):
    return jax.shard_map(
        on_device,
        mesh=mesh,
        in_specs=(
            P(None, "dir", "bl"),
            P("dir", None, None, "bl"),
            P(None, None, "bl"),
            P(None, "bl"),
            P(),
            P(),
            P(),
        ),
        out_specs=(P(None, None, "bl"), P(None, "dir", "bl")),
        check_vma=False,
    )
```

```python
import functools

import jax
import jax.numpy as jnp
from jax import lax
from jax.sharding import PartitionSpec as P
from jax.experimental import pallas as pl
from jax.experimental.pallas import tpu as pltpu

MESH_ID = pl.DeviceIdType.MESH

LM_ITERS = 2
SOLVED = 4


def matrix_entry(mat, i, j):
    return (mat[4 * i + 2 * j], mat[4 * i + 2 * j + 1])


def matmul_two(left, right):
    pieces = []
    for i in (0, 1):
        for j in (0, 1):
            left_r0, left_i0 = matrix_entry(left, i, 0)
            left_r1, left_i1 = matrix_entry(left, i, 1)
            right_r0, right_i0 = matrix_entry(right, 0, j)
            right_r1, right_i1 = matrix_entry(right, 1, j)
            pieces.append(
                left_r0 * right_r0 - left_i0 * right_i0 + left_r1 * right_r1 - left_i1 * right_i1
            )
            pieces.append(
                left_r0 * right_i0 + left_i0 * right_r0 + left_r1 * right_i1 + left_i1 * right_r1
            )
    return jnp.stack(pieces)


def adjoint(mat):
    return jnp.stack([mat[0], -mat[1], mat[4], -mat[5], mat[2], -mat[3], mat[6], -mat[7]])


def apply_gains(gain_p, coher_now, gain_q):
    return matmul_two(matmul_two(gain_p, coher_now), adjoint(gain_q))


def gram_parts(gram):
    return jnp.stack([gram[0], gram[6], gram[2], gram[3]])


def station_terms(gain_p, gain_q, coher_now, target):
    z_rows = matmul_two(coher_now, adjoint(gain_q))
    y_rows = matmul_two(adjoint(coher_now), adjoint(gain_p))
    leading_endpoint = jnp.concatenate(
        [matmul_two(target, adjoint(z_rows)), gram_parts(matmul_two(z_rows, adjoint(z_rows)))], 0
    )
    second = jnp.concatenate(
        [
            matmul_two(adjoint(target), adjoint(y_rows)),
            gram_parts(matmul_two(y_rows, adjoint(y_rows))),
        ],
        0,
    )
    return (jnp.sum(leading_endpoint, axis=1), jnp.sum(second, axis=1))


def solve_station(gathered_sums, gain_now, damp_value):
    numerator = gathered_sums[:8] + damp_value * gain_now
    diag_a = gathered_sums[8] + damp_value
    diag_d = gathered_sums[9] + damp_value
    cross_r = gathered_sums[10]
    cross_i = gathered_sums[11]
    determinant = diag_a * diag_d - cross_r * cross_r - cross_i * cross_i
    zeros_row = jnp.zeros_like(determinant)
    inverse = (
        jnp.stack([diag_d, zeros_row, -cross_r, -cross_i, -cross_r, cross_i, diag_a, zeros_row])
        / determinant
    )
    return matmul_two(numerator, inverse)


def all_reduce_kernel(nb, nz, x_ref, o_ref, r1, r2, r3, s1, q1, s2, q2, s3, q3):
    mz = lax.axis_index("dir")
    mb = lax.axis_index("bl")
    z_peers = [lax.rem(mz + k, nz) for k in range(1, nz)]
    b_peers = [lax.rem(mb + k, nb) for k in range(1, nb)]

    barrier = pltpu.get_barrier_semaphore()
    for p in b_peers:
        pl.semaphore_signal(barrier, 1, device_id=(p, mz), device_id_type=MESH_ID)
    for p in z_peers:
        pl.semaphore_signal(barrier, 1, device_id=(mb, p), device_id_type=MESH_ID)
    pl.semaphore_wait(barrier, (nz - 1) + (nb - 1))

    def exchange(peers, src_of, buf, me, send_sems, recv_sems, device_of):
        sent = []
        for p in peers:
            c = pltpu.make_async_remote_copy(
                src_ref=src_of(p),
                dst_ref=buf.at[me],
                send_sem=send_sems.at[p],
                recv_sem=recv_sems.at[me],
                device_id=device_of(p),
                device_id_type=MESH_ID,
            )
            c.start()
            sent.append(c)
        for p in peers:
            pltpu.make_async_remote_copy(
                src_ref=buf.at[p],
                dst_ref=buf.at[p],
                send_sem=send_sems.at[p],
                recv_sem=recv_sems.at[p],
                device_id=device_of(p),
                device_id_type=MESH_ID,
            ).wait_recv()
        for c in sent:
            c.wait_send()

    exchange(b_peers, lambda p: x_ref.at[p], r1, mb, s1, q1, lambda p: (p, mz))
    own = x_ref[mb]
    for p in b_peers:
        own = own + r1[p]
    r2[mz] = own
    exchange(z_peers, lambda p: r2.at[mz], r2, mz, s2, q2, lambda p: (mb, p))
    total = r2[mz]
    for p in z_peers:
        total = total + r2[p]
    r3[mb] = total
    exchange(b_peers, lambda p: r3.at[mb], r3, mb, s3, q3, lambda p: (p, mz))
    o_ref[...] = r3[...]


def all_reduce(payload, nb, nz):
    chunk_shape = payload.shape[1:]
    return pl.pallas_call(
        functools.partial(all_reduce_kernel, nb, nz),
        out_shape=jax.ShapeDtypeStruct(payload.shape, payload.dtype),
        in_specs=[pl.BlockSpec(memory_space=pltpu.VMEM)],
        out_specs=pl.BlockSpec(memory_space=pltpu.VMEM),
        scratch_shapes=[
            pltpu.VMEM((nb,) + chunk_shape, payload.dtype),
            pltpu.VMEM((nz,) + chunk_shape, payload.dtype),
            pltpu.VMEM((nb,) + chunk_shape, payload.dtype),
            pltpu.SemaphoreType.DMA((nb,)),
            pltpu.SemaphoreType.DMA((nb,)),
            pltpu.SemaphoreType.DMA((nz,)),
            pltpu.SemaphoreType.DMA((nz,)),
            pltpu.SemaphoreType.DMA((nb,)),
            pltpu.SemaphoreType.DMA((nb,)),
        ],
        compiler_params=pltpu.CompilerParams(collective_id=0, has_side_effects=True),
    )(payload)


def station_sum(rows, nz, nb):
    width = rows.shape[0] * 16
    padded = jnp.pad(rows, ((0, 0), (0, 16 - rows.shape[1])))
    summed = all_reduce(padded.reshape(nb, width // (nb * 128), 128), nb, nz)
    return summed.reshape(rows.shape[0], 16)[:, : rows.shape[1]]


def on_device(visibilities, coherencies, gain_offsets, stations, solve_order, counts, damping):
    identity = jnp.zeros((8,), jnp.float32).at[0].set(1.0).at[6].set(1.0)
    start = lax.all_gather(gain_offsets, "bl", axis=2, tiled=True) + identity[None, :, None]
    groups = lax.axis_size("bl")
    nz = lax.axis_size("dir")
    total_channels = coherencies.shape[2]
    station_count = start.shape[2]
    damping_factor = visibilities.shape[2] * groups * total_channels / station_count
    coher_all = lax.all_to_all(coherencies, "dir", 2, 0, tiled=True)
    ends_p = jnp.take(start, stations[0], axis=2)
    ends_q = jnp.take(start, stations[1], axis=2)
    gain_p = jnp.transpose(ends_p, (1, 0, 2))[:, :, None, :]
    gain_q = jnp.transpose(ends_q, (1, 0, 2))[:, :, None, :]
    coher_f32 = jnp.transpose(coher_all, (1, 0, 2, 3)).astype(jnp.float32)
    first_model = jnp.sum(apply_gains(gain_p, coher_f32, gain_q), axis=1)
    first_residual = visibilities - first_model

    def direction_model(gain_now, coher_now):
        gain_p = jnp.take(gain_now, stations[0], axis=1)[:, None, :]
        gain_q = jnp.take(gain_now, stations[1], axis=1)[:, None, :]
        return apply_gains(gain_p, coher_now, gain_q)

    def sweep(step_index, state):
        gain_table, residual = state
        which = solve_order[step_index]
        coher_now = lax.dynamic_index_in_dim(coher_all, which, 0, keepdims=False).astype(
            jnp.float32
        )
        damp_value = damping[which].astype(jnp.float32) * damping_factor
        gain_start = gain_table[which]
        target = residual + direction_model(gain_start, coher_now)

        def iterate(round_index, gain_now):
            gain_p = jnp.take(gain_now, stations[0], axis=1)[:, None, :]
            gain_q = jnp.take(gain_now, stations[1], axis=1)[:, None, :]
            leading_endpoint, second = station_terms(gain_p, gain_q, coher_now, target)
            local_rows = jax.ops.segment_sum(
                leading_endpoint.T, stations[0], station_count
            ) + jax.ops.segment_sum(second.T, stations[1], station_count)
            gathered_sums = station_sum(local_rows, nz, groups).T
            return solve_station(gathered_sums, gain_now, damp_value)

        rounds = jnp.clip(counts[which], 0, LM_ITERS)
        gain_final = lax.fori_loop(0, rounds, iterate, gain_start)
        residual = target - direction_model(gain_final, coher_now)
        return (gain_table.at[which].set(gain_final), residual)

    gain_table, residual = lax.fori_loop(0, SOLVED, sweep, (start, first_residual))
    own_width = station_count // groups
    gains = lax.dynamic_slice_in_dim(gain_table, lax.axis_index("bl") * own_width, own_width, 2)
    return (gains, residual)


def solution(mesh):
    return jax.shard_map(
        on_device,
        mesh=mesh,
        in_specs=(
            P(None, "dir", "bl"),
            P("dir", None, None, "bl"),
            P(None, None, "bl"),
            P(None, "bl"),
            P(),
            P(),
            P(),
        ),
        out_specs=(P(None, None, "bl"), P(None, "dir", "bl")),
        check_vma=False,
    )
```

```python
import functools

import jax
import jax.numpy as jnp
from jax import lax
from jax.sharding import PartitionSpec as P
from jax.experimental import pallas as pl
from jax.experimental.pallas import tpu as pltpu

MESH_ID = pl.DeviceIdType.MESH

LM_ITERS = 2
SOLVED = 4


def matrix_entry(mat, i, j):
    return (mat[4 * i + 2 * j], mat[4 * i + 2 * j + 1])


def matmul_two(left, right):
    pieces = []
    for i in (0, 1):
        for j in (0, 1):
            left_r0, left_i0 = matrix_entry(left, i, 0)
            left_r1, left_i1 = matrix_entry(left, i, 1)
            right_r0, right_i0 = matrix_entry(right, 0, j)
            right_r1, right_i1 = matrix_entry(right, 1, j)
            pieces.append(
                left_r0 * right_r0 - left_i0 * right_i0 + left_r1 * right_r1 - left_i1 * right_i1
            )
            pieces.append(
                left_r0 * right_i0 + left_i0 * right_r0 + left_r1 * right_i1 + left_i1 * right_r1
            )
    return jnp.stack(pieces)


def adjoint(mat):
    return jnp.stack([mat[0], -mat[1], mat[4], -mat[5], mat[2], -mat[3], mat[6], -mat[7]])


def apply_gains(gain_p, coher_now, gain_q):
    return matmul_two(matmul_two(gain_p, coher_now), adjoint(gain_q))


def gram_parts(gram):
    return jnp.stack([gram[0], gram[6], gram[2], gram[3]])


def station_terms(gain_p, gain_q, coher_now, target):
    z_rows = matmul_two(coher_now, adjoint(gain_q))
    y_rows = matmul_two(adjoint(coher_now), adjoint(gain_p))
    leading_endpoint = jnp.concatenate(
        [matmul_two(target, adjoint(z_rows)), gram_parts(matmul_two(z_rows, adjoint(z_rows)))], 0
    )
    second = jnp.concatenate(
        [
            matmul_two(adjoint(target), adjoint(y_rows)),
            gram_parts(matmul_two(y_rows, adjoint(y_rows))),
        ],
        0,
    )
    return (jnp.sum(leading_endpoint, axis=1), jnp.sum(second, axis=1))


def solve_station(gathered_sums, gain_now, damp_value):
    numerator = gathered_sums[:8] + damp_value * gain_now
    diag_a = gathered_sums[8] + damp_value
    diag_d = gathered_sums[9] + damp_value
    cross_r = gathered_sums[10]
    cross_i = gathered_sums[11]
    determinant = diag_a * diag_d - cross_r * cross_r - cross_i * cross_i
    zeros_row = jnp.zeros_like(determinant)
    inverse = (
        jnp.stack([diag_d, zeros_row, -cross_r, -cross_i, -cross_r, cross_i, diag_a, zeros_row])
        / determinant
    )
    return matmul_two(numerator, inverse)


def split_three(x):
    hi = x.astype(jnp.bfloat16)
    rest = x - hi.astype(jnp.float32)
    mid = rest.astype(jnp.bfloat16)
    lo = (rest - mid.astype(jnp.float32)).astype(jnp.bfloat16)
    return (hi, mid, lo)


def gather_cols(parts, onehot):
    out = None
    for part in parts:
        term = jnp.dot(part, onehot, preferred_element_type=jnp.float32)
        out = term if out is None else out + term
    return out


def scatter_cols(values, onehot):
    out = None
    for part in split_three(values):
        term = lax.dot_general(
            part, onehot, (((1,), (1,)), ((), ())), preferred_element_type=jnp.float32
        )
        out = term if out is None else out + term
    return out


def rows_of(x):
    return [x[i : i + 1, :] for i in range(x.shape[0])]


def round_kernel(
    nb, nz, gain_ref, target_ref, coher_ref, onehot_p_ref, onehot_q_ref, damp_ref, o_ref,
    pay, r1, r2, r3, s1, q1, s2, q2, s3, q3,
):
    mz = lax.axis_index("dir")
    mb = lax.axis_index("bl")
    z_peers = [lax.rem(mz + k, nz) for k in range(1, nz)]
    b_peers = [lax.rem(mb + k, nb) for k in range(1, nb)]

    barrier = pltpu.get_barrier_semaphore()
    for p in b_peers:
        pl.semaphore_signal(barrier, 1, device_id=(p, mz), device_id_type=MESH_ID)
    for p in z_peers:
        pl.semaphore_signal(barrier, 1, device_id=(mb, p), device_id_type=MESH_ID)

    gain_now = gain_ref[...]
    parts = split_three(gain_now)
    gain_p = rows_of(gather_cols(parts, onehot_p_ref[...]))
    gain_q = rows_of(gather_cols(parts, onehot_q_ref[...]))
    coher_now = rows_of(coher_ref[...])
    target = rows_of(target_ref[...])
    z_rows = matmul_rows(coher_now, adjoint_rows(gain_q))
    y_rows = matmul_rows(adjoint_rows(coher_now), adjoint_rows(gain_p))
    zero_row = jnp.zeros_like(target[0])
    leading = (
        matmul_rows(target, adjoint_rows(z_rows))
        + gram_rows(matmul_rows(z_rows, adjoint_rows(z_rows)))
        + [zero_row] * 4
    )
    second = (
        matmul_rows(adjoint_rows(target), adjoint_rows(y_rows))
        + gram_rows(matmul_rows(y_rows, adjoint_rows(y_rows)))
        + [zero_row] * 4
    )
    sums = scatter_cols(jnp.concatenate(leading, 0), onehot_p_ref[...]) + scatter_cols(
        jnp.concatenate(second, 0), onehot_q_ref[...]
    )
    groups = sums.shape[1] // 128
    pairs = sums.shape[0] // 2
    per = pay.shape[1]
    for g in range(groups):
        for h in range(pairs):
            slab = g * pairs + h
            pay[slab // per, slab % per] = sums[2 * h : 2 * h + 2, 128 * g : 128 * g + 128]

    pl.semaphore_wait(barrier, (nz - 1) + (nb - 1))

    def exchange(peers, src_of, buf, me, send_sems, recv_sems, device_of):
        sent = []
        for p in peers:
            c = pltpu.make_async_remote_copy(
                src_ref=src_of(p),
                dst_ref=buf.at[me],
                send_sem=send_sems.at[p],
                recv_sem=recv_sems.at[me],
                device_id=device_of(p),
                device_id_type=MESH_ID,
            )
            c.start()
            sent.append(c)
        for p in peers:
            pltpu.make_async_remote_copy(
                src_ref=buf.at[p],
                dst_ref=buf.at[p],
                send_sem=send_sems.at[p],
                recv_sem=recv_sems.at[p],
                device_id=device_of(p),
                device_id_type=MESH_ID,
            ).wait_recv()
        for c in sent:
            c.wait_send()

    exchange(b_peers, lambda p: pay.at[p], r1, mb, s1, q1, lambda p: (p, mz))
    own = pay[mb]
    for p in b_peers:
        own = own + r1[p]
    r2[mz] = own
    exchange(z_peers, lambda p: r2.at[mz], r2, mz, s2, q2, lambda p: (mb, p))
    total = r2[mz]
    for p in z_peers:
        total = total + r2[p]
    r3[mb] = total
    exchange(b_peers, lambda p: r3.at[mb], r3, mb, s3, q3, lambda p: (p, mz))

    gathered = []
    for h in range(pairs):
        for t in range(2):
            pieces = []
            for g in range(groups):
                slab = g * pairs + h
                pieces.append(r3[slab // per, slab % per, t : t + 1, :])
            gathered.append(jnp.concatenate(pieces, 1))
    damp_value = damp_ref[0, 0]
    gain_rows = rows_of(gain_now)
    numerator = [gathered[i] + damp_value * gain_rows[i] for i in range(8)]
    diag_a = gathered[8] + damp_value
    diag_d = gathered[9] + damp_value
    cross_r = gathered[10]
    cross_i = gathered[11]
    determinant = diag_a * diag_d - cross_r * cross_r - cross_i * cross_i
    zeros_row = jnp.zeros_like(determinant)
    inverse = [
        v / determinant
        for v in (diag_d, zeros_row, -cross_r, -cross_i, -cross_r, cross_i, diag_a, zeros_row)
    ]
    o_ref[...] = jnp.concatenate(matmul_rows(numerator, inverse), 0)


def matmul_rows(left, right):
    pieces = []
    for i in (0, 1):
        for j in (0, 1):
            left_r0, left_i0 = left[4 * i], left[4 * i + 1]
            left_r1, left_i1 = left[4 * i + 2], left[4 * i + 3]
            right_r0, right_i0 = right[2 * j], right[2 * j + 1]
            right_r1, right_i1 = right[4 + 2 * j], right[4 + 2 * j + 1]
            pieces.append(
                left_r0 * right_r0 - left_i0 * right_i0 + left_r1 * right_r1 - left_i1 * right_i1
            )
            pieces.append(
                left_r0 * right_i0 + left_i0 * right_r0 + left_r1 * right_i1 + left_i1 * right_r1
            )
    return pieces


def adjoint_rows(mat):
    return [mat[0], -mat[1], mat[4], -mat[5], mat[2], -mat[3], mat[6], -mat[7]]


def gram_rows(gram):
    return [gram[0], gram[6], gram[2], gram[3]]


def damped_round(gain_now, target, coher_now, onehot_p, onehot_q, damp_value, nb, nz):
    stations = gain_now.shape[1]
    per = (16 * stations) // (nb * 2 * 128)
    vmem = pl.BlockSpec(memory_space=pltpu.VMEM)
    return pl.pallas_call(
        functools.partial(round_kernel, nb, nz),
        out_shape=jax.ShapeDtypeStruct(gain_now.shape, gain_now.dtype),
        in_specs=[vmem] * 5 + [pl.BlockSpec(memory_space=pltpu.SMEM)],
        out_specs=vmem,
        scratch_shapes=[
            pltpu.VMEM((nb, per, 2, 128), jnp.float32),
            pltpu.VMEM((nb, per, 2, 128), jnp.float32),
            pltpu.VMEM((nz, per, 2, 128), jnp.float32),
            pltpu.VMEM((nb, per, 2, 128), jnp.float32),
            pltpu.SemaphoreType.DMA((nb,)),
            pltpu.SemaphoreType.DMA((nb,)),
            pltpu.SemaphoreType.DMA((nz,)),
            pltpu.SemaphoreType.DMA((nz,)),
            pltpu.SemaphoreType.DMA((nb,)),
            pltpu.SemaphoreType.DMA((nb,)),
        ],
        compiler_params=pltpu.CompilerParams(collective_id=0, has_side_effects=True),
    )(gain_now, target, coher_now, onehot_p, onehot_q, damp_value.reshape(1, 1))


def on_device(visibilities, coherencies, gain_offsets, stations, solve_order, counts, damping):
    identity = jnp.zeros((8,), jnp.float32).at[0].set(1.0).at[6].set(1.0)
    start = lax.all_gather(gain_offsets, "bl", axis=2, tiled=True) + identity[None, :, None]
    groups = lax.axis_size("bl")
    nz = lax.axis_size("dir")
    total_channels = coherencies.shape[2]
    station_count = start.shape[2]
    damping_factor = visibilities.shape[2] * groups * total_channels / station_count
    coher_all = lax.all_to_all(coherencies, "dir", 2, 0, tiled=True)
    ends_p = jnp.take(start, stations[0], axis=2)
    ends_q = jnp.take(start, stations[1], axis=2)
    gain_p = jnp.transpose(ends_p, (1, 0, 2))[:, :, None, :]
    gain_q = jnp.transpose(ends_q, (1, 0, 2))[:, :, None, :]
    coher_f32 = jnp.transpose(coher_all, (1, 0, 2, 3)).astype(jnp.float32)
    first_model = jnp.sum(apply_gains(gain_p, coher_f32, gain_q), axis=1)
    first_residual = visibilities - first_model

    station_ids = lax.broadcasted_iota(jnp.int32, (station_count, stations.shape[1]), 0)
    onehot_p = (station_ids == stations[0][None, :]).astype(jnp.bfloat16)
    onehot_q = (station_ids == stations[1][None, :]).astype(jnp.bfloat16)

    def direction_model(gain_now, coher_now):
        gain_p = jnp.take(gain_now, stations[0], axis=1)[:, None, :]
        gain_q = jnp.take(gain_now, stations[1], axis=1)[:, None, :]
        return apply_gains(gain_p, coher_now, gain_q)

    def sweep(step_index, state):
        gain_table, residual = state
        which = solve_order[step_index]
        coher_now = lax.dynamic_index_in_dim(coher_all, which, 0, keepdims=False).astype(
            jnp.float32
        )
        damp_value = damping[which].astype(jnp.float32) * damping_factor
        gain_start = gain_table[which]
        target = residual + direction_model(gain_start, coher_now)

        def iterate(round_index, gain_now):
            return damped_round(
                gain_now, target[:, 0, :], coher_now[:, 0, :], onehot_p, onehot_q, damp_value,
                groups, nz,
            )

        rounds = jnp.clip(counts[which], 0, LM_ITERS)
        gain_final = lax.fori_loop(0, rounds, iterate, gain_start)
        residual = target - direction_model(gain_final, coher_now)
        return (gain_table.at[which].set(gain_final), residual)

    gain_table, residual = lax.fori_loop(0, SOLVED, sweep, (start, first_residual))
    own_width = station_count // groups
    gains = lax.dynamic_slice_in_dim(gain_table, lax.axis_index("bl") * own_width, own_width, 2)
    return (gains, residual)


def solution(mesh):
    return jax.shard_map(
        on_device,
        mesh=mesh,
        in_specs=(
            P(None, "dir", "bl"),
            P("dir", None, None, "bl"),
            P(None, None, "bl"),
            P(None, "bl"),
            P(),
            P(),
            P(),
        ),
        out_specs=(P(None, None, "bl"), P(None, "dir", "bl")),
        check_vma=False,
    )
```

```python
import functools

import jax
import jax.numpy as jnp
from jax import lax
from jax.sharding import PartitionSpec as P
from jax.experimental import pallas as pl
from jax.experimental.pallas import tpu as pltpu

MESH_ID = pl.DeviceIdType.MESH

LM_ITERS = 2
SOLVED = 4


def matrix_entry(mat, i, j):
    return (mat[4 * i + 2 * j], mat[4 * i + 2 * j + 1])


def matmul_two(left, right):
    pieces = []
    for i in (0, 1):
        for j in (0, 1):
            left_r0, left_i0 = matrix_entry(left, i, 0)
            left_r1, left_i1 = matrix_entry(left, i, 1)
            right_r0, right_i0 = matrix_entry(right, 0, j)
            right_r1, right_i1 = matrix_entry(right, 1, j)
            pieces.append(
                left_r0 * right_r0 - left_i0 * right_i0 + left_r1 * right_r1 - left_i1 * right_i1
            )
            pieces.append(
                left_r0 * right_i0 + left_i0 * right_r0 + left_r1 * right_i1 + left_i1 * right_r1
            )
    return jnp.stack(pieces)


def adjoint(mat):
    return jnp.stack([mat[0], -mat[1], mat[4], -mat[5], mat[2], -mat[3], mat[6], -mat[7]])


def apply_gains(gain_p, coher_now, gain_q):
    return matmul_two(matmul_two(gain_p, coher_now), adjoint(gain_q))


def gram_parts(gram):
    return jnp.stack([gram[0], gram[6], gram[2], gram[3]])


def station_terms(gain_p, gain_q, coher_now, target):
    z_rows = matmul_two(coher_now, adjoint(gain_q))
    y_rows = matmul_two(adjoint(coher_now), adjoint(gain_p))
    leading_endpoint = jnp.concatenate(
        [matmul_two(target, adjoint(z_rows)), gram_parts(matmul_two(z_rows, adjoint(z_rows)))], 0
    )
    second = jnp.concatenate(
        [
            matmul_two(adjoint(target), adjoint(y_rows)),
            gram_parts(matmul_two(y_rows, adjoint(y_rows))),
        ],
        0,
    )
    return (jnp.sum(leading_endpoint, axis=1), jnp.sum(second, axis=1))


def solve_station(gathered_sums, gain_now, damp_value):
    numerator = gathered_sums[:8] + damp_value * gain_now
    diag_a = gathered_sums[8] + damp_value
    diag_d = gathered_sums[9] + damp_value
    cross_r = gathered_sums[10]
    cross_i = gathered_sums[11]
    determinant = diag_a * diag_d - cross_r * cross_r - cross_i * cross_i
    zeros_row = jnp.zeros_like(determinant)
    inverse = (
        jnp.stack([diag_d, zeros_row, -cross_r, -cross_i, -cross_r, cross_i, diag_a, zeros_row])
        / determinant
    )
    return matmul_two(numerator, inverse)


def split_three(x):
    hi = x.astype(jnp.bfloat16)
    rest = x - hi.astype(jnp.float32)
    mid = rest.astype(jnp.bfloat16)
    lo = (rest - mid.astype(jnp.float32)).astype(jnp.bfloat16)
    return (hi, mid, lo)


def gather_cols(parts, onehot):
    out = None
    for part in parts:
        term = jnp.dot(part, onehot, preferred_element_type=jnp.float32)
        out = term if out is None else out + term
    return out


def scatter_cols(values, onehot):
    out = None
    for part in split_three(values):
        term = lax.dot_general(
            part, onehot, (((1,), (1,)), ((), ())), preferred_element_type=jnp.float32
        )
        out = term if out is None else out + term
    return out


def rows_of(x):
    return [x[i : i + 1, :] for i in range(x.shape[0])]


def round_kernel(
    nb, nz, gain_ref, target_ref, coher_ref, onehot_p_ref, onehot_q_ref, damp_ref, o_ref,
    pay, r1, r2, r3, s1, q1, s2, q2, s3, q3,
):
    mz = lax.axis_index("dir")
    mb = lax.axis_index("bl")
    z_peers = [lax.rem(mz + k, nz) for k in range(1, nz)]
    b_peers = [lax.rem(mb + k, nb) for k in range(1, nb)]

    barrier = pltpu.get_barrier_semaphore()
    for p in b_peers:
        pl.semaphore_signal(barrier, 1, device_id=(p, mz), device_id_type=MESH_ID)
    for p in z_peers:
        pl.semaphore_signal(barrier, 1, device_id=(mb, p), device_id_type=MESH_ID)

    gain_now = gain_ref[...]
    parts = split_three(gain_now)
    gain_p = rows_of(gather_cols(parts, onehot_p_ref[...]))
    gain_q = rows_of(gather_cols(parts, onehot_q_ref[...]))
    coher_now = rows_of(coher_ref[...])
    target = rows_of(target_ref[...])
    z_rows = matmul_rows(coher_now, adjoint_rows(gain_q))
    y_rows = matmul_rows(adjoint_rows(coher_now), adjoint_rows(gain_p))
    zero_row = jnp.zeros_like(target[0])
    leading = (
        matmul_rows(target, adjoint_rows(z_rows))
        + gram_rows(matmul_rows(z_rows, adjoint_rows(z_rows)))
        + [zero_row] * 4
    )
    second = (
        matmul_rows(adjoint_rows(target), adjoint_rows(y_rows))
        + gram_rows(matmul_rows(y_rows, adjoint_rows(y_rows)))
        + [zero_row] * 4
    )
    sums = scatter_cols(jnp.concatenate(leading, 0), onehot_p_ref[...]) + scatter_cols(
        jnp.concatenate(second, 0), onehot_q_ref[...]
    )
    groups = sums.shape[1] // 128
    pairs = sums.shape[0] // 2
    per = pay.shape[1]
    for g in range(groups):
        for h in range(pairs):
            slab = g * pairs + h
            pay[slab // per, slab % per] = sums[2 * h : 2 * h + 2, 128 * g : 128 * g + 128]

    pl.semaphore_wait(barrier, (nz - 1) + (nb - 1))

    def exchange(peers, src_of, buf, me, send_sems, recv_sems, device_of):
        sent = []
        for p in peers:
            c = pltpu.make_async_remote_copy(
                src_ref=src_of(p),
                dst_ref=buf.at[me],
                send_sem=send_sems.at[p],
                recv_sem=recv_sems.at[me],
                device_id=device_of(p),
                device_id_type=MESH_ID,
            )
            c.start()
            sent.append(c)
        for p in peers:
            pltpu.make_async_remote_copy(
                src_ref=buf.at[p],
                dst_ref=buf.at[p],
                send_sem=send_sems.at[p],
                recv_sem=recv_sems.at[p],
                device_id=device_of(p),
                device_id_type=MESH_ID,
            ).wait_recv()
        for c in sent:
            c.wait_send()

    exchange(b_peers, lambda p: pay.at[p], r1, mb, s1, q1, lambda p: (p, mz))
    own = pay[mb]
    for p in b_peers:
        own = own + r1[p]
    r2[mz] = own
    exchange(z_peers, lambda p: r2.at[mz], r2, mz, s2, q2, lambda p: (mb, p))
    total = r2[mz]
    for p in z_peers:
        total = total + r2[p]
    r3[mb] = total
    exchange(b_peers, lambda p: r3.at[mb], r3, mb, s3, q3, lambda p: (p, mz))

    gathered = []
    for h in range(pairs):
        for t in range(2):
            pieces = []
            for g in range(groups):
                slab = g * pairs + h
                pieces.append(r3[slab // per, slab % per, t : t + 1, :])
            gathered.append(jnp.concatenate(pieces, 1))
    damp_value = damp_ref[0, 0]
    gain_rows = rows_of(gain_now)
    numerator = [gathered[i] + damp_value * gain_rows[i] for i in range(8)]
    diag_a = gathered[8] + damp_value
    diag_d = gathered[9] + damp_value
    cross_r = gathered[10]
    cross_i = gathered[11]
    determinant = diag_a * diag_d - cross_r * cross_r - cross_i * cross_i
    zeros_row = jnp.zeros_like(determinant)
    inverse = [
        v / determinant
        for v in (diag_d, zeros_row, -cross_r, -cross_i, -cross_r, cross_i, diag_a, zeros_row)
    ]
    o_ref[...] = jnp.concatenate(matmul_rows(numerator, inverse), 0)


def matmul_rows(left, right):
    pieces = []
    for i in (0, 1):
        for j in (0, 1):
            left_r0, left_i0 = left[4 * i], left[4 * i + 1]
            left_r1, left_i1 = left[4 * i + 2], left[4 * i + 3]
            right_r0, right_i0 = right[2 * j], right[2 * j + 1]
            right_r1, right_i1 = right[4 + 2 * j], right[4 + 2 * j + 1]
            pieces.append(
                left_r0 * right_r0 - left_i0 * right_i0 + left_r1 * right_r1 - left_i1 * right_i1
            )
            pieces.append(
                left_r0 * right_i0 + left_i0 * right_r0 + left_r1 * right_i1 + left_i1 * right_r1
            )
    return pieces


def adjoint_rows(mat):
    return [mat[0], -mat[1], mat[4], -mat[5], mat[2], -mat[3], mat[6], -mat[7]]


def gram_rows(gram):
    return [gram[0], gram[6], gram[2], gram[3]]


def damped_round(gain_now, target, coher_now, onehot_p, onehot_q, damp_value, nb, nz):
    stations = gain_now.shape[1]
    per = (16 * stations) // (nb * 2 * 128)
    vmem = pl.BlockSpec(memory_space=pltpu.VMEM)
    return pl.pallas_call(
        functools.partial(round_kernel, nb, nz),
        out_shape=jax.ShapeDtypeStruct(gain_now.shape, gain_now.dtype),
        in_specs=[vmem] * 5 + [pl.BlockSpec(memory_space=pltpu.SMEM)],
        out_specs=vmem,
        scratch_shapes=[
            pltpu.VMEM((nb, per, 2, 128), jnp.float32),
            pltpu.VMEM((nb, per, 2, 128), jnp.float32),
            pltpu.VMEM((nz, per, 2, 128), jnp.float32),
            pltpu.VMEM((nb, per, 2, 128), jnp.float32),
            pltpu.SemaphoreType.DMA((nb,)),
            pltpu.SemaphoreType.DMA((nb,)),
            pltpu.SemaphoreType.DMA((nz,)),
            pltpu.SemaphoreType.DMA((nz,)),
            pltpu.SemaphoreType.DMA((nb,)),
            pltpu.SemaphoreType.DMA((nb,)),
        ],
        compiler_params=pltpu.CompilerParams(collective_id=0, has_side_effects=True),
    )(gain_now, target, coher_now, onehot_p, onehot_q, damp_value.reshape(1, 1))


def on_device(visibilities, coherencies, gain_offsets, stations, solve_order, counts, damping):
    identity = jnp.zeros((8,), jnp.float32).at[0].set(1.0).at[6].set(1.0)
    groups = lax.axis_size("bl")
    copies = jnp.broadcast_to(gain_offsets[None], (groups,) + gain_offsets.shape)
    blocks = lax.all_to_all(copies, "bl", 0, 0, tiled=True)
    offsets = jnp.transpose(blocks, (1, 2, 0, 3)).reshape(
        gain_offsets.shape[:2] + (groups * gain_offsets.shape[2],)
    )
    start = offsets + identity[None, :, None]
    nz = lax.axis_size("dir")
    total_channels = coherencies.shape[2]
    station_count = start.shape[2]
    damping_factor = visibilities.shape[2] * groups * total_channels / station_count
    coher_all = lax.all_to_all(coherencies, "dir", 2, 0, tiled=True)
    ends_p = jnp.take(start, stations[0], axis=2)
    ends_q = jnp.take(start, stations[1], axis=2)
    gain_p = jnp.transpose(ends_p, (1, 0, 2))[:, :, None, :]
    gain_q = jnp.transpose(ends_q, (1, 0, 2))[:, :, None, :]
    coher_f32 = jnp.transpose(coher_all, (1, 0, 2, 3)).astype(jnp.float32)
    first_model = jnp.sum(apply_gains(gain_p, coher_f32, gain_q), axis=1)
    first_residual = visibilities - first_model

    station_ids = lax.broadcasted_iota(jnp.int32, (station_count, stations.shape[1]), 0)
    onehot_p = (station_ids == stations[0][None, :]).astype(jnp.bfloat16)
    onehot_q = (station_ids == stations[1][None, :]).astype(jnp.bfloat16)

    def direction_model(gain_now, coher_now):
        gain_p = jnp.take(gain_now, stations[0], axis=1)[:, None, :]
        gain_q = jnp.take(gain_now, stations[1], axis=1)[:, None, :]
        return apply_gains(gain_p, coher_now, gain_q)

    def sweep(step_index, state):
        gain_table, residual = state
        which = solve_order[step_index]
        coher_now = lax.dynamic_index_in_dim(coher_all, which, 0, keepdims=False).astype(
            jnp.float32
        )
        damp_value = damping[which].astype(jnp.float32) * damping_factor
        gain_start = gain_table[which]
        target = residual + direction_model(gain_start, coher_now)

        def iterate(round_index, gain_now):
            return damped_round(
                gain_now, target[:, 0, :], coher_now[:, 0, :], onehot_p, onehot_q, damp_value,
                groups, nz,
            )

        rounds = jnp.clip(counts[which], 0, LM_ITERS)
        gain_final = lax.fori_loop(0, rounds, iterate, gain_start)
        residual = target - direction_model(gain_final, coher_now)
        return (gain_table.at[which].set(gain_final), residual)

    gain_table, residual = lax.fori_loop(0, SOLVED, sweep, (start, first_residual))
    own_width = station_count // groups
    gains = lax.dynamic_slice_in_dim(gain_table, lax.axis_index("bl") * own_width, own_width, 2)
    return (gains, residual)


def solution(mesh):
    return jax.shard_map(
        on_device,
        mesh=mesh,
        in_specs=(
            P(None, "dir", "bl"),
            P("dir", None, None, "bl"),
            P(None, None, "bl"),
            P(None, "bl"),
            P(),
            P(),
            P(),
        ),
        out_specs=(P(None, None, "bl"), P(None, "dir", "bl")),
        check_vma=False,
    )
```

```python
import functools

import jax
import jax.numpy as jnp
from jax import lax
from jax.sharding import PartitionSpec as P
from jax.experimental import pallas as pl
from jax.experimental.pallas import tpu as pltpu

MESH_ID = pl.DeviceIdType.MESH

LM_ITERS = 2
SOLVED = 4


def matrix_entry(mat, i, j):
    return (mat[4 * i + 2 * j], mat[4 * i + 2 * j + 1])


def matmul_two(left, right):
    pieces = []
    for i in (0, 1):
        for j in (0, 1):
            left_r0, left_i0 = matrix_entry(left, i, 0)
            left_r1, left_i1 = matrix_entry(left, i, 1)
            right_r0, right_i0 = matrix_entry(right, 0, j)
            right_r1, right_i1 = matrix_entry(right, 1, j)
            pieces.append(
                left_r0 * right_r0 - left_i0 * right_i0 + left_r1 * right_r1 - left_i1 * right_i1
            )
            pieces.append(
                left_r0 * right_i0 + left_i0 * right_r0 + left_r1 * right_i1 + left_i1 * right_r1
            )
    return jnp.stack(pieces)


def adjoint(mat):
    return jnp.stack([mat[0], -mat[1], mat[4], -mat[5], mat[2], -mat[3], mat[6], -mat[7]])


def apply_gains(gain_p, coher_now, gain_q):
    return matmul_two(matmul_two(gain_p, coher_now), adjoint(gain_q))


def gram_parts(gram):
    return jnp.stack([gram[0], gram[6], gram[2], gram[3]])


def station_terms(gain_p, gain_q, coher_now, target):
    z_rows = matmul_two(coher_now, adjoint(gain_q))
    y_rows = matmul_two(adjoint(coher_now), adjoint(gain_p))
    leading_endpoint = jnp.concatenate(
        [matmul_two(target, adjoint(z_rows)), gram_parts(matmul_two(z_rows, adjoint(z_rows)))], 0
    )
    second = jnp.concatenate(
        [
            matmul_two(adjoint(target), adjoint(y_rows)),
            gram_parts(matmul_two(y_rows, adjoint(y_rows))),
        ],
        0,
    )
    return (jnp.sum(leading_endpoint, axis=1), jnp.sum(second, axis=1))


def solve_station(gathered_sums, gain_now, damp_value):
    numerator = gathered_sums[:8] + damp_value * gain_now
    diag_a = gathered_sums[8] + damp_value
    diag_d = gathered_sums[9] + damp_value
    cross_r = gathered_sums[10]
    cross_i = gathered_sums[11]
    determinant = diag_a * diag_d - cross_r * cross_r - cross_i * cross_i
    zeros_row = jnp.zeros_like(determinant)
    inverse = (
        jnp.stack([diag_d, zeros_row, -cross_r, -cross_i, -cross_r, cross_i, diag_a, zeros_row])
        / determinant
    )
    return matmul_two(numerator, inverse)


def split_three(x):
    hi = x.astype(jnp.bfloat16)
    rest = x - hi.astype(jnp.float32)
    mid = rest.astype(jnp.bfloat16)
    lo = (rest - mid.astype(jnp.float32)).astype(jnp.bfloat16)
    return (hi, mid, lo)


def gather_cols(parts, onehot):
    out = None
    for part in parts:
        term = jnp.dot(part, onehot, preferred_element_type=jnp.float32)
        out = term if out is None else out + term
    return out


def scatter_cols(values, onehot):
    out = None
    for part in split_three(values):
        term = lax.dot_general(
            part, onehot, (((1,), (1,)), ((), ())), preferred_element_type=jnp.float32
        )
        out = term if out is None else out + term
    return out


def rows_of(x):
    return [x[i : i + 1, :] for i in range(x.shape[0])]


def round_kernel(
    nb, nz, gain_ref, target_ref, coher_ref, onehot_p_ref, onehot_q_ref, damp_ref, o_ref,
    pay, r1, r2, r3, s1, q1, s2, q2, s3, q3,
):
    mz = lax.axis_index("dir")
    mb = lax.axis_index("bl")
    z_peers = [lax.rem(mz + k, nz) for k in range(1, nz)]
    b_peers = [lax.rem(mb + k, nb) for k in range(1, nb)]

    barrier = pltpu.get_barrier_semaphore()
    for p in b_peers:
        pl.semaphore_signal(barrier, 1, device_id=(p, mz), device_id_type=MESH_ID)
    for p in z_peers:
        pl.semaphore_signal(barrier, 1, device_id=(mb, p), device_id_type=MESH_ID)

    gain_now = gain_ref[...]
    parts = split_three(gain_now)
    gain_p = rows_of(gather_cols(parts, onehot_p_ref[...]))
    gain_q = rows_of(gather_cols(parts, onehot_q_ref[...]))
    coher_now = rows_of(coher_ref[...])
    target = rows_of(target_ref[...])
    z_rows = matmul_rows(coher_now, adjoint_rows(gain_q))
    y_rows = matmul_rows(adjoint_rows(coher_now), adjoint_rows(gain_p))
    zero_row = jnp.zeros_like(target[0])
    leading = (
        matmul_rows(target, adjoint_rows(z_rows))
        + gram_rows(matmul_rows(z_rows, adjoint_rows(z_rows)))
        + [zero_row] * 4
    )
    second = (
        matmul_rows(adjoint_rows(target), adjoint_rows(y_rows))
        + gram_rows(matmul_rows(y_rows, adjoint_rows(y_rows)))
        + [zero_row] * 4
    )
    sums = scatter_cols(jnp.concatenate(leading, 0), onehot_p_ref[...]) + scatter_cols(
        jnp.concatenate(second, 0), onehot_q_ref[...]
    )
    groups = sums.shape[1] // 128
    pairs = sums.shape[0] // 2
    per = pay.shape[1]
    for g in range(groups):
        for h in range(pairs):
            slab = g * pairs + h
            pay[slab // per, slab % per] = sums[2 * h : 2 * h + 2, 128 * g : 128 * g + 128]

    pl.semaphore_wait(barrier, (nz - 1) + (nb - 1))

    def exchange(peers, src_of, buf, me, send_sems, recv_sems, device_of):
        sent = []
        for p in peers:
            c = pltpu.make_async_remote_copy(
                src_ref=src_of(p),
                dst_ref=buf.at[me],
                send_sem=send_sems.at[p],
                recv_sem=recv_sems.at[me],
                device_id=device_of(p),
                device_id_type=MESH_ID,
            )
            c.start()
            sent.append(c)
        for p in peers:
            pltpu.make_async_remote_copy(
                src_ref=buf.at[p],
                dst_ref=buf.at[p],
                send_sem=send_sems.at[p],
                recv_sem=recv_sems.at[p],
                device_id=device_of(p),
                device_id_type=MESH_ID,
            ).wait_recv()
        for c in sent:
            c.wait_send()

    exchange(b_peers, lambda p: pay.at[p], r1, mb, s1, q1, lambda p: (p, mz))
    own = pay[mb]
    for p in b_peers:
        own = own + r1[p]
    r2[mz] = own
    exchange(z_peers, lambda p: r2.at[mz], r2, mz, s2, q2, lambda p: (mb, p))
    total = r2[mz]
    for p in z_peers:
        total = total + r2[p]
    r3[mb] = total
    exchange(b_peers, lambda p: r3.at[mb], r3, mb, s3, q3, lambda p: (p, mz))

    gathered = []
    for h in range(pairs):
        for t in range(2):
            pieces = []
            for g in range(groups):
                slab = g * pairs + h
                pieces.append(r3[slab // per, slab % per, t : t + 1, :])
            gathered.append(jnp.concatenate(pieces, 1))
    damp_value = damp_ref[0, 0]
    gain_rows = rows_of(gain_now)
    numerator = [gathered[i] + damp_value * gain_rows[i] for i in range(8)]
    diag_a = gathered[8] + damp_value
    diag_d = gathered[9] + damp_value
    cross_r = gathered[10]
    cross_i = gathered[11]
    determinant = diag_a * diag_d - cross_r * cross_r - cross_i * cross_i
    zeros_row = jnp.zeros_like(determinant)
    inverse = [
        v / determinant
        for v in (diag_d, zeros_row, -cross_r, -cross_i, -cross_r, cross_i, diag_a, zeros_row)
    ]
    o_ref[...] = jnp.concatenate(matmul_rows(numerator, inverse), 0)


def matmul_rows(left, right):
    pieces = []
    for i in (0, 1):
        for j in (0, 1):
            left_r0, left_i0 = left[4 * i], left[4 * i + 1]
            left_r1, left_i1 = left[4 * i + 2], left[4 * i + 3]
            right_r0, right_i0 = right[2 * j], right[2 * j + 1]
            right_r1, right_i1 = right[4 + 2 * j], right[4 + 2 * j + 1]
            pieces.append(
                left_r0 * right_r0 - left_i0 * right_i0 + left_r1 * right_r1 - left_i1 * right_i1
            )
            pieces.append(
                left_r0 * right_i0 + left_i0 * right_r0 + left_r1 * right_i1 + left_i1 * right_r1
            )
    return pieces


def adjoint_rows(mat):
    return [mat[0], -mat[1], mat[4], -mat[5], mat[2], -mat[3], mat[6], -mat[7]]


def gram_rows(gram):
    return [gram[0], gram[6], gram[2], gram[3]]


def damped_round(gain_now, target, coher_now, onehot_p, onehot_q, damp_value, nb, nz):
    stations = gain_now.shape[1]
    per = (16 * stations) // (nb * 2 * 128)
    vmem = pl.BlockSpec(memory_space=pltpu.VMEM)
    return pl.pallas_call(
        functools.partial(round_kernel, nb, nz),
        out_shape=jax.ShapeDtypeStruct(gain_now.shape, gain_now.dtype),
        in_specs=[vmem] * 5 + [pl.BlockSpec(memory_space=pltpu.SMEM)],
        out_specs=vmem,
        scratch_shapes=[
            pltpu.VMEM((nb, per, 2, 128), jnp.float32),
            pltpu.VMEM((nb, per, 2, 128), jnp.float32),
            pltpu.VMEM((nz, per, 2, 128), jnp.float32),
            pltpu.VMEM((nb, per, 2, 128), jnp.float32),
            pltpu.SemaphoreType.DMA((nb,)),
            pltpu.SemaphoreType.DMA((nb,)),
            pltpu.SemaphoreType.DMA((nz,)),
            pltpu.SemaphoreType.DMA((nz,)),
            pltpu.SemaphoreType.DMA((nb,)),
            pltpu.SemaphoreType.DMA((nb,)),
        ],
        compiler_params=pltpu.CompilerParams(collective_id=0, has_side_effects=True),
    )(gain_now, target, coher_now, onehot_p, onehot_q, damp_value.reshape(1, 1))


def prologue_kernel(nb, nz, coh_ref, gain_ref, coh_out, gain_out, coh_buf, gain_buf, s1, q1, s2, q2):
    mz = lax.axis_index("dir")
    mb = lax.axis_index("bl")
    z_peers = [lax.rem(mz + k, nz) for k in range(1, nz)]
    b_peers = [lax.rem(mb + k, nb) for k in range(1, nb)]

    barrier = pltpu.get_barrier_semaphore()
    for p in b_peers:
        pl.semaphore_signal(barrier, 1, device_id=(p, mz), device_id_type=MESH_ID)
    for p in z_peers:
        pl.semaphore_signal(barrier, 1, device_id=(mb, p), device_id_type=MESH_ID)
    pl.semaphore_wait(barrier, (nz - 1) + (nb - 1))

    sent = []
    for p in z_peers:
        c = pltpu.make_async_remote_copy(
            src_ref=coh_ref.at[p],
            dst_ref=coh_buf.at[mz],
            send_sem=s1.at[p],
            recv_sem=q1.at[mz],
            device_id=(mb, p),
            device_id_type=MESH_ID,
        )
        c.start()
        sent.append(c)
    for p in b_peers:
        c = pltpu.make_async_remote_copy(
            src_ref=gain_ref,
            dst_ref=gain_buf.at[mb],
            send_sem=s2.at[p],
            recv_sem=q2.at[mb],
            device_id=(p, mz),
            device_id_type=MESH_ID,
        )
        c.start()
        sent.append(c)
    coh_buf[mz] = coh_ref[mz]
    gain_buf[mb] = gain_ref[...]
    for p in z_peers:
        pltpu.make_async_remote_copy(
            src_ref=coh_buf.at[p],
            dst_ref=coh_buf.at[p],
            send_sem=s1.at[p],
            recv_sem=q1.at[p],
            device_id=(mb, p),
            device_id_type=MESH_ID,
        ).wait_recv()
    for p in b_peers:
        pltpu.make_async_remote_copy(
            src_ref=gain_buf.at[p],
            dst_ref=gain_buf.at[p],
            send_sem=s2.at[p],
            recv_sem=q2.at[p],
            device_id=(p, mz),
            device_id_type=MESH_ID,
        ).wait_recv()
    for c in sent:
        c.wait_send()
    coh_out[...] = coh_buf[...]
    gain_out[...] = gain_buf[...]


def exchange_inputs(coh_by_channel, gain_block, nb, nz):
    vmem = pl.BlockSpec(memory_space=pltpu.VMEM)
    coh_shape = (nz,) + coh_by_channel.shape[1:]
    gain_shape = (nb,) + gain_block.shape
    return pl.pallas_call(
        functools.partial(prologue_kernel, nb, nz),
        out_shape=(
            jax.ShapeDtypeStruct(coh_shape, coh_by_channel.dtype),
            jax.ShapeDtypeStruct(gain_shape, gain_block.dtype),
        ),
        in_specs=[vmem, vmem],
        out_specs=(vmem, vmem),
        scratch_shapes=[
            pltpu.VMEM(coh_shape, coh_by_channel.dtype),
            pltpu.VMEM(gain_shape, gain_block.dtype),
            pltpu.SemaphoreType.DMA((nz,)),
            pltpu.SemaphoreType.DMA((nz,)),
            pltpu.SemaphoreType.DMA((nb,)),
            pltpu.SemaphoreType.DMA((nb,)),
        ],
        compiler_params=pltpu.CompilerParams(collective_id=1, has_side_effects=True),
    )(coh_by_channel, gain_block)


def on_device(visibilities, coherencies, gain_offsets, stations, solve_order, counts, damping):
    identity = jnp.zeros((8,), jnp.float32).at[0].set(1.0).at[6].set(1.0)
    groups = lax.axis_size("bl")
    nz = lax.axis_size("dir")
    owned, _, channels_all, width = coherencies.shape
    by_channel = jnp.transpose(coherencies, (2, 0, 1, 3)).reshape(channels_all, owned * 8, width)
    coh_recv, gain_recv = exchange_inputs(
        by_channel, gain_offsets.reshape(-1, 128), groups, nz
    )
    direction_total = gain_offsets.shape[0]
    offsets = jnp.transpose(
        gain_recv.reshape((groups,) + gain_offsets.shape), (1, 2, 0, 3)
    ).reshape(direction_total, 8, groups * gain_offsets.shape[2])
    start = offsets + identity[None, :, None]
    coher_all = coh_recv.reshape(nz * owned, 8, 1, width)
    total_channels = coherencies.shape[2]
    station_count = start.shape[2]
    damping_factor = visibilities.shape[2] * groups * total_channels / station_count
    ends_p = jnp.take(start, stations[0], axis=2)
    ends_q = jnp.take(start, stations[1], axis=2)
    gain_p = jnp.transpose(ends_p, (1, 0, 2))[:, :, None, :]
    gain_q = jnp.transpose(ends_q, (1, 0, 2))[:, :, None, :]
    coher_f32 = jnp.transpose(coher_all, (1, 0, 2, 3)).astype(jnp.float32)
    first_model = jnp.sum(apply_gains(gain_p, coher_f32, gain_q), axis=1)
    first_residual = visibilities - first_model

    station_ids = lax.broadcasted_iota(jnp.int32, (station_count, stations.shape[1]), 0)
    onehot_p = (station_ids == stations[0][None, :]).astype(jnp.bfloat16)
    onehot_q = (station_ids == stations[1][None, :]).astype(jnp.bfloat16)

    def direction_model(gain_now, coher_now):
        gain_p = jnp.take(gain_now, stations[0], axis=1)[:, None, :]
        gain_q = jnp.take(gain_now, stations[1], axis=1)[:, None, :]
        return apply_gains(gain_p, coher_now, gain_q)

    def sweep(step_index, state):
        gain_table, residual = state
        which = solve_order[step_index]
        coher_now = lax.dynamic_index_in_dim(coher_all, which, 0, keepdims=False).astype(
            jnp.float32
        )
        damp_value = damping[which].astype(jnp.float32) * damping_factor
        gain_start = gain_table[which]
        target = residual + direction_model(gain_start, coher_now)

        def iterate(round_index, gain_now):
            return damped_round(
                gain_now, target[:, 0, :], coher_now[:, 0, :], onehot_p, onehot_q, damp_value,
                groups, nz,
            )

        rounds = jnp.clip(counts[which], 0, LM_ITERS)
        gain_final = lax.fori_loop(0, rounds, iterate, gain_start)
        residual = target - direction_model(gain_final, coher_now)
        return (gain_table.at[which].set(gain_final), residual)

    gain_table, residual = lax.fori_loop(0, SOLVED, sweep, (start, first_residual))
    own_width = station_count // groups
    gains = lax.dynamic_slice_in_dim(gain_table, lax.axis_index("bl") * own_width, own_width, 2)
    return (gains, residual)


def solution(mesh):
    return jax.shard_map(
        on_device,
        mesh=mesh,
        in_specs=(
            P(None, "dir", "bl"),
            P("dir", None, None, "bl"),
            P(None, None, "bl"),
            P(None, "bl"),
            P(),
            P(),
            P(),
        ),
        out_specs=(P(None, None, "bl"), P(None, "dir", "bl")),
        check_vma=False,
    )
```

```python
import functools

import jax
import jax.numpy as jnp
from jax import lax
from jax.sharding import PartitionSpec as P
from jax.experimental import pallas as pl
from jax.experimental.pallas import tpu as pltpu

MESH_ID = pl.DeviceIdType.MESH

LM_ITERS = 2
SOLVED = 4


def matrix_entry(mat, i, j):
    return (mat[4 * i + 2 * j], mat[4 * i + 2 * j + 1])


def matmul_two(left, right):
    pieces = []
    for i in (0, 1):
        for j in (0, 1):
            left_r0, left_i0 = matrix_entry(left, i, 0)
            left_r1, left_i1 = matrix_entry(left, i, 1)
            right_r0, right_i0 = matrix_entry(right, 0, j)
            right_r1, right_i1 = matrix_entry(right, 1, j)
            pieces.append(
                left_r0 * right_r0 - left_i0 * right_i0 + left_r1 * right_r1 - left_i1 * right_i1
            )
            pieces.append(
                left_r0 * right_i0 + left_i0 * right_r0 + left_r1 * right_i1 + left_i1 * right_r1
            )
    return jnp.stack(pieces)


def adjoint(mat):
    return jnp.stack([mat[0], -mat[1], mat[4], -mat[5], mat[2], -mat[3], mat[6], -mat[7]])


def apply_gains(gain_p, coher_now, gain_q):
    return matmul_two(matmul_two(gain_p, coher_now), adjoint(gain_q))


def gram_parts(gram):
    return jnp.stack([gram[0], gram[6], gram[2], gram[3]])


def station_terms(gain_p, gain_q, coher_now, target):
    z_rows = matmul_two(coher_now, adjoint(gain_q))
    y_rows = matmul_two(adjoint(coher_now), adjoint(gain_p))
    leading_endpoint = jnp.concatenate(
        [matmul_two(target, adjoint(z_rows)), gram_parts(matmul_two(z_rows, adjoint(z_rows)))], 0
    )
    second = jnp.concatenate(
        [
            matmul_two(adjoint(target), adjoint(y_rows)),
            gram_parts(matmul_two(y_rows, adjoint(y_rows))),
        ],
        0,
    )
    return (jnp.sum(leading_endpoint, axis=1), jnp.sum(second, axis=1))


def solve_station(gathered_sums, gain_now, damp_value):
    numerator = gathered_sums[:8] + damp_value * gain_now
    diag_a = gathered_sums[8] + damp_value
    diag_d = gathered_sums[9] + damp_value
    cross_r = gathered_sums[10]
    cross_i = gathered_sums[11]
    determinant = diag_a * diag_d - cross_r * cross_r - cross_i * cross_i
    zeros_row = jnp.zeros_like(determinant)
    inverse = (
        jnp.stack([diag_d, zeros_row, -cross_r, -cross_i, -cross_r, cross_i, diag_a, zeros_row])
        / determinant
    )
    return matmul_two(numerator, inverse)


def split_three(x):
    hi = x.astype(jnp.bfloat16)
    rest = x - hi.astype(jnp.float32)
    mid = rest.astype(jnp.bfloat16)
    lo = (rest - mid.astype(jnp.float32)).astype(jnp.bfloat16)
    return (hi, mid, lo)


def gather_cols(parts, onehot):
    out = None
    for part in parts:
        term = jnp.dot(part, onehot, preferred_element_type=jnp.float32)
        out = term if out is None else out + term
    return out


def scatter_cols(values, onehot):
    out = None
    for part in split_three(values):
        term = lax.dot_general(
            part, onehot, (((1,), (1,)), ((), ())), preferred_element_type=jnp.float32
        )
        out = term if out is None else out + term
    return out


def rows_of(x):
    return [x[i : i + 1, :] for i in range(x.shape[0])]


def model_rows(gain_parts, coher_now, onehot_p, onehot_q):
    gain_p = rows_of(gather_cols(gain_parts, onehot_p))
    gain_q = rows_of(gather_cols(gain_parts, onehot_q))
    return matmul_rows(matmul_rows(gain_p, coher_now), adjoint_rows(gain_q))


def round_kernel(
    nb, nz, gain_ref, start_ref, residual_ref, coher_ref, onehot_p_ref, onehot_q_ref, damp_ref,
    o_ref, res_out, pay, r1, r2, r3, s1, q1, s2, q2, s3, q3,
):
    mz = lax.axis_index("dir")
    mb = lax.axis_index("bl")
    z_peers = [lax.rem(mz + k, nz) for k in range(1, nz)]
    b_peers = [lax.rem(mb + k, nb) for k in range(1, nb)]

    barrier = pltpu.get_barrier_semaphore()
    for p in b_peers:
        pl.semaphore_signal(barrier, 1, device_id=(p, mz), device_id_type=MESH_ID)
    for p in z_peers:
        pl.semaphore_signal(barrier, 1, device_id=(mb, p), device_id_type=MESH_ID)

    gain_now = gain_ref[...]
    parts = split_three(gain_now)
    gain_p = rows_of(gather_cols(parts, onehot_p_ref[...]))
    gain_q = rows_of(gather_cols(parts, onehot_q_ref[...]))
    coher_now = rows_of(coher_ref[...])
    start_model = model_rows(
        split_three(start_ref[...]), coher_now, onehot_p_ref[...], onehot_q_ref[...]
    )
    residual_rows = rows_of(residual_ref[...])
    target = [residual_rows[i] + start_model[i] for i in range(8)]
    z_rows = matmul_rows(coher_now, adjoint_rows(gain_q))
    y_rows = matmul_rows(adjoint_rows(coher_now), adjoint_rows(gain_p))
    zero_row = jnp.zeros_like(target[0])
    leading = (
        matmul_rows(target, adjoint_rows(z_rows))
        + gram_rows(matmul_rows(z_rows, adjoint_rows(z_rows)))
        + [zero_row] * 4
    )
    second = (
        matmul_rows(adjoint_rows(target), adjoint_rows(y_rows))
        + gram_rows(matmul_rows(y_rows, adjoint_rows(y_rows)))
        + [zero_row] * 4
    )
    sums = scatter_cols(jnp.concatenate(leading, 0), onehot_p_ref[...]) + scatter_cols(
        jnp.concatenate(second, 0), onehot_q_ref[...]
    )
    groups = sums.shape[1] // 128
    pairs = sums.shape[0] // 2
    per = pay.shape[1]
    for g in range(groups):
        for h in range(pairs):
            slab = g * pairs + h
            pay[slab // per, slab % per] = sums[2 * h : 2 * h + 2, 128 * g : 128 * g + 128]

    pl.semaphore_wait(barrier, (nz - 1) + (nb - 1))

    def exchange(peers, src_of, buf, me, send_sems, recv_sems, device_of):
        sent = []
        for p in peers:
            c = pltpu.make_async_remote_copy(
                src_ref=src_of(p),
                dst_ref=buf.at[me],
                send_sem=send_sems.at[p],
                recv_sem=recv_sems.at[me],
                device_id=device_of(p),
                device_id_type=MESH_ID,
            )
            c.start()
            sent.append(c)
        for p in peers:
            pltpu.make_async_remote_copy(
                src_ref=buf.at[p],
                dst_ref=buf.at[p],
                send_sem=send_sems.at[p],
                recv_sem=recv_sems.at[p],
                device_id=device_of(p),
                device_id_type=MESH_ID,
            ).wait_recv()
        for c in sent:
            c.wait_send()

    exchange(b_peers, lambda p: pay.at[p], r1, mb, s1, q1, lambda p: (p, mz))
    own = pay[mb]
    for p in b_peers:
        own = own + r1[p]
    r2[mz] = own
    exchange(z_peers, lambda p: r2.at[mz], r2, mz, s2, q2, lambda p: (mb, p))
    total = r2[mz]
    for p in z_peers:
        total = total + r2[p]
    r3[mb] = total
    exchange(b_peers, lambda p: r3.at[mb], r3, mb, s3, q3, lambda p: (p, mz))

    gathered = []
    for h in range(pairs):
        for t in range(2):
            pieces = []
            for g in range(groups):
                slab = g * pairs + h
                pieces.append(r3[slab // per, slab % per, t : t + 1, :])
            gathered.append(jnp.concatenate(pieces, 1))
    damp_value = damp_ref[0, 0]
    gain_rows = rows_of(gain_now)
    numerator = [gathered[i] + damp_value * gain_rows[i] for i in range(8)]
    diag_a = gathered[8] + damp_value
    diag_d = gathered[9] + damp_value
    cross_r = gathered[10]
    cross_i = gathered[11]
    determinant = diag_a * diag_d - cross_r * cross_r - cross_i * cross_i
    zeros_row = jnp.zeros_like(determinant)
    inverse = [
        v / determinant
        for v in (diag_d, zeros_row, -cross_r, -cross_i, -cross_r, cross_i, diag_a, zeros_row)
    ]
    updated = jnp.concatenate(matmul_rows(numerator, inverse), 0)
    o_ref[...] = updated
    final_model = model_rows(
        split_three(updated), coher_now, onehot_p_ref[...], onehot_q_ref[...]
    )
    res_out[...] = jnp.concatenate([target[i] - final_model[i] for i in range(8)], 0)


def matmul_rows(left, right):
    pieces = []
    for i in (0, 1):
        for j in (0, 1):
            left_r0, left_i0 = left[4 * i], left[4 * i + 1]
            left_r1, left_i1 = left[4 * i + 2], left[4 * i + 3]
            right_r0, right_i0 = right[2 * j], right[2 * j + 1]
            right_r1, right_i1 = right[4 + 2 * j], right[4 + 2 * j + 1]
            pieces.append(
                left_r0 * right_r0 - left_i0 * right_i0 + left_r1 * right_r1 - left_i1 * right_i1
            )
            pieces.append(
                left_r0 * right_i0 + left_i0 * right_r0 + left_r1 * right_i1 + left_i1 * right_r1
            )
    return pieces


def adjoint_rows(mat):
    return [mat[0], -mat[1], mat[4], -mat[5], mat[2], -mat[3], mat[6], -mat[7]]


def gram_rows(gram):
    return [gram[0], gram[6], gram[2], gram[3]]


def damped_round(
    gain_now, gain_start, residual, coher_now, onehot_p, onehot_q, damp_value, nb, nz
):
    stations = gain_now.shape[1]
    per = (16 * stations) // (nb * 2 * 128)
    vmem = pl.BlockSpec(memory_space=pltpu.VMEM)
    return pl.pallas_call(
        functools.partial(round_kernel, nb, nz),
        out_shape=(
            jax.ShapeDtypeStruct(gain_now.shape, gain_now.dtype),
            jax.ShapeDtypeStruct(residual.shape, residual.dtype),
        ),
        in_specs=[vmem] * 6 + [pl.BlockSpec(memory_space=pltpu.SMEM)],
        out_specs=(vmem, vmem),
        scratch_shapes=[
            pltpu.VMEM((nb, per, 2, 128), jnp.float32),
            pltpu.VMEM((nb, per, 2, 128), jnp.float32),
            pltpu.VMEM((nz, per, 2, 128), jnp.float32),
            pltpu.VMEM((nb, per, 2, 128), jnp.float32),
            pltpu.SemaphoreType.DMA((nb,)),
            pltpu.SemaphoreType.DMA((nb,)),
            pltpu.SemaphoreType.DMA((nz,)),
            pltpu.SemaphoreType.DMA((nz,)),
            pltpu.SemaphoreType.DMA((nb,)),
            pltpu.SemaphoreType.DMA((nb,)),
        ],
        compiler_params=pltpu.CompilerParams(collective_id=0, has_side_effects=True),
    )(gain_now, gain_start, residual, coher_now, onehot_p, onehot_q, damp_value.reshape(1, 1))


def prologue_kernel(nb, nz, coh_ref, gain_ref, coh_out, gain_out, coh_buf, gain_buf, s1, q1, s2, q2):
    mz = lax.axis_index("dir")
    mb = lax.axis_index("bl")
    z_peers = [lax.rem(mz + k, nz) for k in range(1, nz)]
    b_peers = [lax.rem(mb + k, nb) for k in range(1, nb)]

    barrier = pltpu.get_barrier_semaphore()
    for p in b_peers:
        pl.semaphore_signal(barrier, 1, device_id=(p, mz), device_id_type=MESH_ID)
    for p in z_peers:
        pl.semaphore_signal(barrier, 1, device_id=(mb, p), device_id_type=MESH_ID)
    pl.semaphore_wait(barrier, (nz - 1) + (nb - 1))

    sent = []
    for p in z_peers:
        c = pltpu.make_async_remote_copy(
            src_ref=coh_ref.at[p],
            dst_ref=coh_buf.at[mz],
            send_sem=s1.at[p],
            recv_sem=q1.at[mz],
            device_id=(mb, p),
            device_id_type=MESH_ID,
        )
        c.start()
        sent.append(c)
    for p in b_peers:
        c = pltpu.make_async_remote_copy(
            src_ref=gain_ref,
            dst_ref=gain_buf.at[mb],
            send_sem=s2.at[p],
            recv_sem=q2.at[mb],
            device_id=(p, mz),
            device_id_type=MESH_ID,
        )
        c.start()
        sent.append(c)
    coh_buf[mz] = coh_ref[mz]
    gain_buf[mb] = gain_ref[...]
    for p in z_peers:
        pltpu.make_async_remote_copy(
            src_ref=coh_buf.at[p],
            dst_ref=coh_buf.at[p],
            send_sem=s1.at[p],
            recv_sem=q1.at[p],
            device_id=(mb, p),
            device_id_type=MESH_ID,
        ).wait_recv()
    for p in b_peers:
        pltpu.make_async_remote_copy(
            src_ref=gain_buf.at[p],
            dst_ref=gain_buf.at[p],
            send_sem=s2.at[p],
            recv_sem=q2.at[p],
            device_id=(p, mz),
            device_id_type=MESH_ID,
        ).wait_recv()
    for c in sent:
        c.wait_send()
    coh_out[...] = coh_buf[...]
    gain_out[...] = gain_buf[...]


def exchange_inputs(coh_by_channel, gain_block, nb, nz):
    vmem = pl.BlockSpec(memory_space=pltpu.VMEM)
    coh_shape = (nz,) + coh_by_channel.shape[1:]
    gain_shape = (nb,) + gain_block.shape
    return pl.pallas_call(
        functools.partial(prologue_kernel, nb, nz),
        out_shape=(
            jax.ShapeDtypeStruct(coh_shape, coh_by_channel.dtype),
            jax.ShapeDtypeStruct(gain_shape, gain_block.dtype),
        ),
        in_specs=[vmem, vmem],
        out_specs=(vmem, vmem),
        scratch_shapes=[
            pltpu.VMEM(coh_shape, coh_by_channel.dtype),
            pltpu.VMEM(gain_shape, gain_block.dtype),
            pltpu.SemaphoreType.DMA((nz,)),
            pltpu.SemaphoreType.DMA((nz,)),
            pltpu.SemaphoreType.DMA((nb,)),
            pltpu.SemaphoreType.DMA((nb,)),
        ],
        compiler_params=pltpu.CompilerParams(collective_id=1, has_side_effects=True),
    )(coh_by_channel, gain_block)


def on_device(visibilities, coherencies, gain_offsets, stations, solve_order, counts, damping):
    identity = jnp.zeros((8,), jnp.float32).at[0].set(1.0).at[6].set(1.0)
    groups = lax.axis_size("bl")
    nz = lax.axis_size("dir")
    owned, _, channels_all, width = coherencies.shape
    by_channel = jnp.transpose(coherencies, (2, 0, 1, 3)).reshape(channels_all, owned * 8, width)
    coh_recv, gain_recv = exchange_inputs(
        by_channel, gain_offsets.reshape(-1, 128), groups, nz
    )
    direction_total = gain_offsets.shape[0]
    offsets = jnp.transpose(
        gain_recv.reshape((groups,) + gain_offsets.shape), (1, 2, 0, 3)
    ).reshape(direction_total, 8, groups * gain_offsets.shape[2])
    start = offsets + identity[None, :, None]
    coher_all = coh_recv.reshape(nz * owned, 8, 1, width)
    total_channels = coherencies.shape[2]
    station_count = start.shape[2]
    damping_factor = visibilities.shape[2] * groups * total_channels / station_count
    ends_p = jnp.take(start, stations[0], axis=2)
    ends_q = jnp.take(start, stations[1], axis=2)
    gain_p = jnp.transpose(ends_p, (1, 0, 2))[:, :, None, :]
    gain_q = jnp.transpose(ends_q, (1, 0, 2))[:, :, None, :]
    coher_f32 = jnp.transpose(coher_all, (1, 0, 2, 3)).astype(jnp.float32)
    first_model = jnp.sum(apply_gains(gain_p, coher_f32, gain_q), axis=1)
    first_residual = visibilities - first_model

    station_ids = lax.broadcasted_iota(jnp.int32, (station_count, stations.shape[1]), 0)
    onehot_p = (station_ids == stations[0][None, :]).astype(jnp.bfloat16)
    onehot_q = (station_ids == stations[1][None, :]).astype(jnp.bfloat16)

    def direction_model(gain_now, coher_now):
        gain_p = jnp.take(gain_now, stations[0], axis=1)[:, None, :]
        gain_q = jnp.take(gain_now, stations[1], axis=1)[:, None, :]
        return apply_gains(gain_p, coher_now, gain_q)

    def sweep(step_index, state):
        gain_table, residual = state
        which = solve_order[step_index]
        coher_now = lax.dynamic_index_in_dim(coher_all, which, 0, keepdims=False)[:, 0, :].astype(
            jnp.float32
        )
        damp_value = damping[which].astype(jnp.float32) * damping_factor
        gain_start = gain_table[which]
        residual_before = residual[:, 0, :]

        def iterate(round_index, carry):
            gain_now, _ = carry
            return damped_round(
                gain_now, gain_start, residual_before, coher_now, onehot_p, onehot_q,
                damp_value, groups, nz,
            )

        rounds = jnp.clip(counts[which], 0, LM_ITERS)
        gain_final, residual_after = lax.fori_loop(
            0, rounds, iterate, (gain_start, residual_before)
        )
        return (gain_table.at[which].set(gain_final), residual_after[:, None, :])

    gain_table, residual = lax.fori_loop(0, SOLVED, sweep, (start, first_residual))
    own_width = station_count // groups
    gains = lax.dynamic_slice_in_dim(gain_table, lax.axis_index("bl") * own_width, own_width, 2)
    return (gains, residual)


def solution(mesh):
    return jax.shard_map(
        on_device,
        mesh=mesh,
        in_specs=(
            P(None, "dir", "bl"),
            P("dir", None, None, "bl"),
            P(None, None, "bl"),
            P(None, "bl"),
            P(),
            P(),
            P(),
        ),
        out_specs=(P(None, None, "bl"), P(None, "dir", "bl")),
        check_vma=False,
    )
```

```python
import functools

import jax
import jax.numpy as jnp
from jax import lax
from jax.sharding import PartitionSpec as P
from jax.experimental import pallas as pl
from jax.experimental.pallas import tpu as pltpu

MESH_ID = pl.DeviceIdType.MESH

LM_ITERS = 2
SOLVED = 4


def matrix_entry(mat, i, j):
    return (mat[4 * i + 2 * j], mat[4 * i + 2 * j + 1])


def matmul_two(left, right):
    pieces = []
    for i in (0, 1):
        for j in (0, 1):
            left_r0, left_i0 = matrix_entry(left, i, 0)
            left_r1, left_i1 = matrix_entry(left, i, 1)
            right_r0, right_i0 = matrix_entry(right, 0, j)
            right_r1, right_i1 = matrix_entry(right, 1, j)
            pieces.append(
                left_r0 * right_r0 - left_i0 * right_i0 + left_r1 * right_r1 - left_i1 * right_i1
            )
            pieces.append(
                left_r0 * right_i0 + left_i0 * right_r0 + left_r1 * right_i1 + left_i1 * right_r1
            )
    return jnp.stack(pieces)


def adjoint(mat):
    return jnp.stack([mat[0], -mat[1], mat[4], -mat[5], mat[2], -mat[3], mat[6], -mat[7]])


def apply_gains(gain_p, coher_now, gain_q):
    return matmul_two(matmul_two(gain_p, coher_now), adjoint(gain_q))


def gram_parts(gram):
    return jnp.stack([gram[0], gram[6], gram[2], gram[3]])


def station_terms(gain_p, gain_q, coher_now, target):
    z_rows = matmul_two(coher_now, adjoint(gain_q))
    y_rows = matmul_two(adjoint(coher_now), adjoint(gain_p))
    leading_endpoint = jnp.concatenate(
        [matmul_two(target, adjoint(z_rows)), gram_parts(matmul_two(z_rows, adjoint(z_rows)))], 0
    )
    second = jnp.concatenate(
        [
            matmul_two(adjoint(target), adjoint(y_rows)),
            gram_parts(matmul_two(y_rows, adjoint(y_rows))),
        ],
        0,
    )
    return (jnp.sum(leading_endpoint, axis=1), jnp.sum(second, axis=1))


def solve_station(gathered_sums, gain_now, damp_value):
    numerator = gathered_sums[:8] + damp_value * gain_now
    diag_a = gathered_sums[8] + damp_value
    diag_d = gathered_sums[9] + damp_value
    cross_r = gathered_sums[10]
    cross_i = gathered_sums[11]
    determinant = diag_a * diag_d - cross_r * cross_r - cross_i * cross_i
    zeros_row = jnp.zeros_like(determinant)
    inverse = (
        jnp.stack([diag_d, zeros_row, -cross_r, -cross_i, -cross_r, cross_i, diag_a, zeros_row])
        / determinant
    )
    return matmul_two(numerator, inverse)


def split_three(x):
    hi = x.astype(jnp.bfloat16)
    rest = x - hi.astype(jnp.float32)
    mid = rest.astype(jnp.bfloat16)
    lo = (rest - mid.astype(jnp.float32)).astype(jnp.bfloat16)
    return (hi, mid, lo)


def gather_cols(parts, onehot):
    out = None
    for part in parts:
        term = jnp.dot(part, onehot, preferred_element_type=jnp.float32)
        out = term if out is None else out + term
    return out


def scatter_cols(values, onehot):
    out = None
    for part in split_three(values):
        term = lax.dot_general(
            part, onehot, (((1,), (1,)), ((), ())), preferred_element_type=jnp.float32
        )
        out = term if out is None else out + term
    return out


def rows_of(x):
    return [x[i : i + 1, :] for i in range(x.shape[0])]


def model_rows(gain_parts, coher_now, onehot_p, onehot_q):
    gain_p = rows_of(gather_cols(gain_parts, onehot_p))
    gain_q = rows_of(gather_cols(gain_parts, onehot_q))
    return matmul_rows(matmul_rows(gain_p, coher_now), adjoint_rows(gain_q))


def round_kernel(
    nb, nz, rounds, gain_ref, start_ref, residual_ref, coher_ref, onehot_p_ref, onehot_q_ref, damp_ref,
    o_ref, res_out, pay, r1, r2, r3, s1, q1, s2, q2, s3, q3,
):
    mz = lax.axis_index("dir")
    mb = lax.axis_index("bl")
    z_peers = [lax.rem(mz + k, nz) for k in range(1, nz)]
    b_peers = [lax.rem(mb + k, nb) for k in range(1, nb)]

    barrier = pltpu.get_barrier_semaphore()
    for p in b_peers:
        pl.semaphore_signal(barrier, 1, device_id=(p, mz), device_id_type=MESH_ID)
    for p in z_peers:
        pl.semaphore_signal(barrier, 1, device_id=(mb, p), device_id_type=MESH_ID)

    coher_now = rows_of(coher_ref[...])
    onehot_p = onehot_p_ref[...]
    onehot_q = onehot_q_ref[...]
    start_model = model_rows(split_three(start_ref[...]), coher_now, onehot_p, onehot_q)
    residual_rows = rows_of(residual_ref[...])
    target = [residual_rows[i] + start_model[i] for i in range(8)]
    damp_value = damp_ref[0, 0]
    groups = None
    pairs = None
    per = pay.shape[1]

    def exchange(peers, src_of, buf, me, send_sems, recv_sems, device_of, r):
        sent = []
        for p in peers:
            c = pltpu.make_async_remote_copy(
                src_ref=src_of(p),
                dst_ref=buf.at[r, me],
                send_sem=send_sems.at[r, p],
                recv_sem=recv_sems.at[r, me],
                device_id=device_of(p),
                device_id_type=MESH_ID,
            )
            c.start()
            sent.append(c)
        for p in peers:
            pltpu.make_async_remote_copy(
                src_ref=buf.at[r, p],
                dst_ref=buf.at[r, p],
                send_sem=send_sems.at[r, p],
                recv_sem=recv_sems.at[r, p],
                device_id=device_of(p),
                device_id_type=MESH_ID,
            ).wait_recv()
        for c in sent:
            c.wait_send()

    def local_sums(gain_now):
        parts = split_three(gain_now)
        gain_p = rows_of(gather_cols(parts, onehot_p))
        gain_q = rows_of(gather_cols(parts, onehot_q))
        z_rows = matmul_rows(coher_now, adjoint_rows(gain_q))
        y_rows = matmul_rows(adjoint_rows(coher_now), adjoint_rows(gain_p))
        zero_row = jnp.zeros_like(target[0])
        leading = (
            matmul_rows(target, adjoint_rows(z_rows))
            + gram_rows(matmul_rows(z_rows, adjoint_rows(z_rows)))
            + [zero_row] * 4
        )
        second = (
            matmul_rows(adjoint_rows(target), adjoint_rows(y_rows))
            + gram_rows(matmul_rows(y_rows, adjoint_rows(y_rows)))
            + [zero_row] * 4
        )
        sums = scatter_cols(jnp.concatenate(leading, 0), onehot_p) + scatter_cols(
            jnp.concatenate(second, 0), onehot_q
        )
        groups = sums.shape[1] // 128
        pairs = sums.shape[0] // 2
        for g in range(groups):
            for h in range(pairs):
                slab = g * pairs + h
                pay[slab // per, slab % per] = sums[2 * h : 2 * h + 2, 128 * g : 128 * g + 128]
        return groups, pairs

    def all_reduce(r):
        exchange(b_peers, lambda p: pay.at[p], r1, mb, s1, q1, lambda p: (p, mz), r)
        own = pay[mb]
        for p in b_peers:
            own = own + r1[r, p]
        r2[r, mz] = own
        exchange(z_peers, lambda p: r2.at[r, mz], r2, mz, s2, q2, lambda p: (mb, p), r)
        total = r2[r, mz]
        for p in z_peers:
            total = total + r2[r, p]
        r3[r, mb] = total
        exchange(b_peers, lambda p: r3.at[r, mb], r3, mb, s3, q3, lambda p: (p, mz), r)

    def solve(gain_now, groups, pairs, r):
        gathered = []
        for h in range(pairs):
            for t in range(2):
                pieces = []
                for g in range(groups):
                    slab = g * pairs + h
                    pieces.append(r3[r, slab // per, slab % per, t : t + 1, :])
                gathered.append(jnp.concatenate(pieces, 1))
        gain_rows = rows_of(gain_now)
        numerator = [gathered[i] + damp_value * gain_rows[i] for i in range(8)]
        diag_a = gathered[8] + damp_value
        diag_d = gathered[9] + damp_value
        cross_r = gathered[10]
        cross_i = gathered[11]
        determinant = diag_a * diag_d - cross_r * cross_r - cross_i * cross_i
        zeros_row = jnp.zeros_like(determinant)
        inverse = [
            v / determinant
            for v in (diag_d, zeros_row, -cross_r, -cross_i, -cross_r, cross_i, diag_a, zeros_row)
        ]
        return jnp.concatenate(matmul_rows(numerator, inverse), 0)

    gain_now = gain_ref[...]
    groups, pairs = local_sums(gain_now)
    pl.semaphore_wait(barrier, (nz - 1) + (nb - 1))
    all_reduce(0)
    gain_now = solve(gain_now, groups, pairs, 0)
    for r in range(1, rounds):
        local_sums(gain_now)
        all_reduce(r)
        gain_now = solve(gain_now, groups, pairs, r)
    o_ref[...] = gain_now
    final_model = model_rows(split_three(gain_now), coher_now, onehot_p, onehot_q)
    res_out[...] = jnp.concatenate([target[i] - final_model[i] for i in range(8)], 0)


def matmul_rows(left, right):
    pieces = []
    for i in (0, 1):
        for j in (0, 1):
            left_r0, left_i0 = left[4 * i], left[4 * i + 1]
            left_r1, left_i1 = left[4 * i + 2], left[4 * i + 3]
            right_r0, right_i0 = right[2 * j], right[2 * j + 1]
            right_r1, right_i1 = right[4 + 2 * j], right[4 + 2 * j + 1]
            pieces.append(
                left_r0 * right_r0 - left_i0 * right_i0 + left_r1 * right_r1 - left_i1 * right_i1
            )
            pieces.append(
                left_r0 * right_i0 + left_i0 * right_r0 + left_r1 * right_i1 + left_i1 * right_r1
            )
    return pieces


def adjoint_rows(mat):
    return [mat[0], -mat[1], mat[4], -mat[5], mat[2], -mat[3], mat[6], -mat[7]]


def gram_rows(gram):
    return [gram[0], gram[6], gram[2], gram[3]]


def damped_rounds(
    rounds, gain_now, gain_start, residual, coher_now, onehot_p, onehot_q, damp_value, nb, nz
):
    stations = gain_now.shape[1]
    per = (16 * stations) // (nb * 2 * 128)
    vmem = pl.BlockSpec(memory_space=pltpu.VMEM)
    return pl.pallas_call(
        functools.partial(round_kernel, nb, nz, rounds),
        out_shape=(
            jax.ShapeDtypeStruct(gain_now.shape, gain_now.dtype),
            jax.ShapeDtypeStruct(residual.shape, residual.dtype),
        ),
        in_specs=[vmem] * 6 + [pl.BlockSpec(memory_space=pltpu.SMEM)],
        out_specs=(vmem, vmem),
        scratch_shapes=[
            pltpu.VMEM((nb, per, 2, 128), jnp.float32),
            pltpu.VMEM((rounds, nb, per, 2, 128), jnp.float32),
            pltpu.VMEM((rounds, nz, per, 2, 128), jnp.float32),
            pltpu.VMEM((rounds, nb, per, 2, 128), jnp.float32),
            pltpu.SemaphoreType.DMA((rounds, nb)),
            pltpu.SemaphoreType.DMA((rounds, nb)),
            pltpu.SemaphoreType.DMA((rounds, nz)),
            pltpu.SemaphoreType.DMA((rounds, nz)),
            pltpu.SemaphoreType.DMA((rounds, nb)),
            pltpu.SemaphoreType.DMA((rounds, nb)),
        ],
        compiler_params=pltpu.CompilerParams(collective_id=2 * rounds, has_side_effects=True),
    )(gain_now, gain_start, residual, coher_now, onehot_p, onehot_q, damp_value.reshape(1, 1))


def prologue_kernel(nb, nz, coh_ref, gain_ref, coh_out, gain_out, coh_buf, gain_buf, s1, q1, s2, q2):
    mz = lax.axis_index("dir")
    mb = lax.axis_index("bl")
    z_peers = [lax.rem(mz + k, nz) for k in range(1, nz)]
    b_peers = [lax.rem(mb + k, nb) for k in range(1, nb)]

    barrier = pltpu.get_barrier_semaphore()
    for p in b_peers:
        pl.semaphore_signal(barrier, 1, device_id=(p, mz), device_id_type=MESH_ID)
    for p in z_peers:
        pl.semaphore_signal(barrier, 1, device_id=(mb, p), device_id_type=MESH_ID)
    pl.semaphore_wait(barrier, (nz - 1) + (nb - 1))

    sent = []
    for p in z_peers:
        c = pltpu.make_async_remote_copy(
            src_ref=coh_ref.at[p],
            dst_ref=coh_buf.at[mz],
            send_sem=s1.at[p],
            recv_sem=q1.at[mz],
            device_id=(mb, p),
            device_id_type=MESH_ID,
        )
        c.start()
        sent.append(c)
    for p in b_peers:
        c = pltpu.make_async_remote_copy(
            src_ref=gain_ref,
            dst_ref=gain_buf.at[mb],
            send_sem=s2.at[p],
            recv_sem=q2.at[mb],
            device_id=(p, mz),
            device_id_type=MESH_ID,
        )
        c.start()
        sent.append(c)
    coh_buf[mz] = coh_ref[mz]
    gain_buf[mb] = gain_ref[...]
    for p in z_peers:
        pltpu.make_async_remote_copy(
            src_ref=coh_buf.at[p],
            dst_ref=coh_buf.at[p],
            send_sem=s1.at[p],
            recv_sem=q1.at[p],
            device_id=(mb, p),
            device_id_type=MESH_ID,
        ).wait_recv()
    for p in b_peers:
        pltpu.make_async_remote_copy(
            src_ref=gain_buf.at[p],
            dst_ref=gain_buf.at[p],
            send_sem=s2.at[p],
            recv_sem=q2.at[p],
            device_id=(p, mz),
            device_id_type=MESH_ID,
        ).wait_recv()
    for c in sent:
        c.wait_send()
    coh_out[...] = coh_buf[...]
    gain_out[...] = gain_buf[...]


def exchange_inputs(coh_by_channel, gain_block, nb, nz):
    vmem = pl.BlockSpec(memory_space=pltpu.VMEM)
    coh_shape = (nz,) + coh_by_channel.shape[1:]
    gain_shape = (nb,) + gain_block.shape
    return pl.pallas_call(
        functools.partial(prologue_kernel, nb, nz),
        out_shape=(
            jax.ShapeDtypeStruct(coh_shape, coh_by_channel.dtype),
            jax.ShapeDtypeStruct(gain_shape, gain_block.dtype),
        ),
        in_specs=[vmem, vmem],
        out_specs=(vmem, vmem),
        scratch_shapes=[
            pltpu.VMEM(coh_shape, coh_by_channel.dtype),
            pltpu.VMEM(gain_shape, gain_block.dtype),
            pltpu.SemaphoreType.DMA((nz,)),
            pltpu.SemaphoreType.DMA((nz,)),
            pltpu.SemaphoreType.DMA((nb,)),
            pltpu.SemaphoreType.DMA((nb,)),
        ],
        compiler_params=pltpu.CompilerParams(collective_id=1, has_side_effects=True),
    )(coh_by_channel, gain_block)


def on_device(visibilities, coherencies, gain_offsets, stations, solve_order, counts, damping):
    identity = jnp.zeros((8,), jnp.float32).at[0].set(1.0).at[6].set(1.0)
    groups = lax.axis_size("bl")
    nz = lax.axis_size("dir")
    owned, _, channels_all, width = coherencies.shape
    by_channel = jnp.transpose(coherencies, (2, 0, 1, 3)).reshape(channels_all, owned * 8, width)
    coh_recv, gain_recv = exchange_inputs(
        by_channel, gain_offsets.reshape(-1, 128), groups, nz
    )
    direction_total = gain_offsets.shape[0]
    offsets = jnp.transpose(
        gain_recv.reshape((groups,) + gain_offsets.shape), (1, 2, 0, 3)
    ).reshape(direction_total, 8, groups * gain_offsets.shape[2])
    start = offsets + identity[None, :, None]
    coher_all = coh_recv.reshape(nz * owned, 8, 1, width)
    total_channels = coherencies.shape[2]
    station_count = start.shape[2]
    damping_factor = visibilities.shape[2] * groups * total_channels / station_count
    ends_p = jnp.take(start, stations[0], axis=2)
    ends_q = jnp.take(start, stations[1], axis=2)
    gain_p = jnp.transpose(ends_p, (1, 0, 2))[:, :, None, :]
    gain_q = jnp.transpose(ends_q, (1, 0, 2))[:, :, None, :]
    coher_f32 = jnp.transpose(coher_all, (1, 0, 2, 3)).astype(jnp.float32)
    first_model = jnp.sum(apply_gains(gain_p, coher_f32, gain_q), axis=1)
    first_residual = visibilities - first_model

    station_ids = lax.broadcasted_iota(jnp.int32, (station_count, stations.shape[1]), 0)
    onehot_p = (station_ids == stations[0][None, :]).astype(jnp.bfloat16)
    onehot_q = (station_ids == stations[1][None, :]).astype(jnp.bfloat16)

    def direction_model(gain_now, coher_now):
        gain_p = jnp.take(gain_now, stations[0], axis=1)[:, None, :]
        gain_q = jnp.take(gain_now, stations[1], axis=1)[:, None, :]
        return apply_gains(gain_p, coher_now, gain_q)

    def sweep(step_index, state):
        gain_table, residual = state
        which = solve_order[step_index]
        coher_now = lax.dynamic_index_in_dim(coher_all, which, 0, keepdims=False)[:, 0, :].astype(
            jnp.float32
        )
        damp_value = damping[which].astype(jnp.float32) * damping_factor
        gain_start = gain_table[which]
        residual_before = residual[:, 0, :]

        def run(rounds):
            def branch(operands):
                if rounds == 0:
                    return (gain_start, residual_before)
                return damped_rounds(
                    rounds, gain_start, gain_start, residual_before, coher_now, onehot_p,
                    onehot_q, damp_value, groups, nz,
                )

            return branch

        rounds = jnp.clip(counts[which], 0, LM_ITERS)
        gain_final, residual_after = lax.switch(
            rounds, [run(r) for r in range(LM_ITERS + 1)], None
        )
        return (gain_table.at[which].set(gain_final), residual_after[:, None, :])

    gain_table, residual = lax.fori_loop(0, SOLVED, sweep, (start, first_residual))
    own_width = station_count // groups
    gains = lax.dynamic_slice_in_dim(gain_table, lax.axis_index("bl") * own_width, own_width, 2)
    return (gains, residual)


def solution(mesh):
    return jax.shard_map(
        on_device,
        mesh=mesh,
        in_specs=(
            P(None, "dir", "bl"),
            P("dir", None, None, "bl"),
            P(None, None, "bl"),
            P(None, "bl"),
            P(),
            P(),
            P(),
        ),
        out_specs=(P(None, None, "bl"), P(None, "dir", "bl")),
        check_vma=False,
    )
```

```python
import functools

import jax
import jax.numpy as jnp
from jax import lax
from jax.sharding import PartitionSpec as P
from jax.experimental import pallas as pl
from jax.experimental.pallas import tpu as pltpu

MESH_ID = pl.DeviceIdType.MESH

LM_ITERS = 2
SOLVED = 4


def matrix_entry(mat, i, j):
    return (mat[4 * i + 2 * j], mat[4 * i + 2 * j + 1])


def matmul_two(left, right):
    pieces = []
    for i in (0, 1):
        for j in (0, 1):
            left_r0, left_i0 = matrix_entry(left, i, 0)
            left_r1, left_i1 = matrix_entry(left, i, 1)
            right_r0, right_i0 = matrix_entry(right, 0, j)
            right_r1, right_i1 = matrix_entry(right, 1, j)
            pieces.append(
                left_r0 * right_r0 - left_i0 * right_i0 + left_r1 * right_r1 - left_i1 * right_i1
            )
            pieces.append(
                left_r0 * right_i0 + left_i0 * right_r0 + left_r1 * right_i1 + left_i1 * right_r1
            )
    return jnp.stack(pieces)


def adjoint(mat):
    return jnp.stack([mat[0], -mat[1], mat[4], -mat[5], mat[2], -mat[3], mat[6], -mat[7]])


def apply_gains(gain_p, coher_now, gain_q):
    return matmul_two(matmul_two(gain_p, coher_now), adjoint(gain_q))


def gram_parts(gram):
    return jnp.stack([gram[0], gram[6], gram[2], gram[3]])


def station_terms(gain_p, gain_q, coher_now, target):
    z_rows = matmul_two(coher_now, adjoint(gain_q))
    y_rows = matmul_two(adjoint(coher_now), adjoint(gain_p))
    leading_endpoint = jnp.concatenate(
        [matmul_two(target, adjoint(z_rows)), gram_parts(matmul_two(z_rows, adjoint(z_rows)))], 0
    )
    second = jnp.concatenate(
        [
            matmul_two(adjoint(target), adjoint(y_rows)),
            gram_parts(matmul_two(y_rows, adjoint(y_rows))),
        ],
        0,
    )
    return (jnp.sum(leading_endpoint, axis=1), jnp.sum(second, axis=1))


def solve_station(gathered_sums, gain_now, damp_value):
    numerator = gathered_sums[:8] + damp_value * gain_now
    diag_a = gathered_sums[8] + damp_value
    diag_d = gathered_sums[9] + damp_value
    cross_r = gathered_sums[10]
    cross_i = gathered_sums[11]
    determinant = diag_a * diag_d - cross_r * cross_r - cross_i * cross_i
    zeros_row = jnp.zeros_like(determinant)
    inverse = (
        jnp.stack([diag_d, zeros_row, -cross_r, -cross_i, -cross_r, cross_i, diag_a, zeros_row])
        / determinant
    )
    return matmul_two(numerator, inverse)


def split_three(x):
    hi = x.astype(jnp.bfloat16)
    rest = x - hi.astype(jnp.float32)
    mid = rest.astype(jnp.bfloat16)
    lo = (rest - mid.astype(jnp.float32)).astype(jnp.bfloat16)
    return (hi, mid, lo)


def gather_cols(parts, onehot):
    out = None
    for part in parts:
        term = jnp.dot(part, onehot, preferred_element_type=jnp.float32)
        out = term if out is None else out + term
    return out


def scatter_cols(values, onehot):
    out = None
    for part in split_three(values):
        term = lax.dot_general(
            part, onehot, (((1,), (1,)), ((), ())), preferred_element_type=jnp.float32
        )
        out = term if out is None else out + term
    return out


def rows_of(x):
    return [x[i : i + 1, :] for i in range(x.shape[0])]


def model_rows(gain_parts, coher_now, onehot_p, onehot_q):
    gain_p = rows_of(gather_cols(gain_parts, onehot_p))
    gain_q = rows_of(gather_cols(gain_parts, onehot_q))
    return matmul_rows(matmul_rows(gain_p, coher_now), adjoint_rows(gain_q))


def round_kernel(
    nb, nz, rounds, which_ref, damp_ref, table_ref, residual_ref, coher_ref, onehot_p_ref,
    onehot_q_ref, o_ref, res_out, pay, r1, r2, r3, s1, q1, s2, q2, s3, q3,
):
    mz = lax.axis_index("dir")
    mb = lax.axis_index("bl")
    z_peers = [lax.rem(mz + k, nz) for k in range(1, nz)]
    b_peers = [lax.rem(mb + k, nb) for k in range(1, nb)]

    barrier = pltpu.get_barrier_semaphore()
    for p in b_peers:
        pl.semaphore_signal(barrier, 1, device_id=(p, mz), device_id_type=MESH_ID)
    for p in z_peers:
        pl.semaphore_signal(barrier, 1, device_id=(mb, p), device_id_type=MESH_ID)

    which = which_ref[0]
    gain_start = table_ref[which]
    coher_now = rows_of(coher_ref[which].astype(jnp.float32))
    onehot_p = onehot_p_ref[...]
    onehot_q = onehot_q_ref[...]
    start_model = model_rows(split_three(gain_start), coher_now, onehot_p, onehot_q)
    residual_rows = rows_of(residual_ref[...])
    target = [residual_rows[i] + start_model[i] for i in range(8)]
    damp_value = damp_ref[0, 0]
    groups = None
    pairs = None
    per = pay.shape[1]

    def exchange(peers, src_of, buf, me, send_sems, recv_sems, device_of, r):
        sent = []
        for p in peers:
            c = pltpu.make_async_remote_copy(
                src_ref=src_of(p),
                dst_ref=buf.at[r, me],
                send_sem=send_sems.at[r, p],
                recv_sem=recv_sems.at[r, me],
                device_id=device_of(p),
                device_id_type=MESH_ID,
            )
            c.start()
            sent.append(c)
        for p in peers:
            pltpu.make_async_remote_copy(
                src_ref=buf.at[r, p],
                dst_ref=buf.at[r, p],
                send_sem=send_sems.at[r, p],
                recv_sem=recv_sems.at[r, p],
                device_id=device_of(p),
                device_id_type=MESH_ID,
            ).wait_recv()
        for c in sent:
            c.wait_send()

    def local_sums(gain_now):
        parts = split_three(gain_now)
        gain_p = rows_of(gather_cols(parts, onehot_p))
        gain_q = rows_of(gather_cols(parts, onehot_q))
        z_rows = matmul_rows(coher_now, adjoint_rows(gain_q))
        y_rows = matmul_rows(adjoint_rows(coher_now), adjoint_rows(gain_p))
        zero_row = jnp.zeros_like(target[0])
        leading = (
            matmul_rows(target, adjoint_rows(z_rows))
            + gram_rows(matmul_rows(z_rows, adjoint_rows(z_rows)))
            + [zero_row] * 4
        )
        second = (
            matmul_rows(adjoint_rows(target), adjoint_rows(y_rows))
            + gram_rows(matmul_rows(y_rows, adjoint_rows(y_rows)))
            + [zero_row] * 4
        )
        sums = scatter_cols(jnp.concatenate(leading, 0), onehot_p) + scatter_cols(
            jnp.concatenate(second, 0), onehot_q
        )
        groups = sums.shape[1] // 128
        pairs = sums.shape[0] // 2
        for g in range(groups):
            for h in range(pairs):
                slab = g * pairs + h
                pay[slab // per, slab % per] = sums[2 * h : 2 * h + 2, 128 * g : 128 * g + 128]
        return groups, pairs

    def all_reduce(r):
        exchange(b_peers, lambda p: pay.at[p], r1, mb, s1, q1, lambda p: (p, mz), r)
        own = pay[mb]
        for p in b_peers:
            own = own + r1[r, p]
        r2[r, mz] = own
        exchange(z_peers, lambda p: r2.at[r, mz], r2, mz, s2, q2, lambda p: (mb, p), r)
        total = r2[r, mz]
        for p in z_peers:
            total = total + r2[r, p]
        r3[r, mb] = total
        exchange(b_peers, lambda p: r3.at[r, mb], r3, mb, s3, q3, lambda p: (p, mz), r)

    def solve(gain_now, groups, pairs, r):
        gathered = []
        for h in range(pairs):
            for t in range(2):
                pieces = []
                for g in range(groups):
                    slab = g * pairs + h
                    pieces.append(r3[r, slab // per, slab % per, t : t + 1, :])
                gathered.append(jnp.concatenate(pieces, 1))
        gain_rows = rows_of(gain_now)
        numerator = [gathered[i] + damp_value * gain_rows[i] for i in range(8)]
        diag_a = gathered[8] + damp_value
        diag_d = gathered[9] + damp_value
        cross_r = gathered[10]
        cross_i = gathered[11]
        determinant = diag_a * diag_d - cross_r * cross_r - cross_i * cross_i
        zeros_row = jnp.zeros_like(determinant)
        inverse = [
            v / determinant
            for v in (diag_d, zeros_row, -cross_r, -cross_i, -cross_r, cross_i, diag_a, zeros_row)
        ]
        return jnp.concatenate(matmul_rows(numerator, inverse), 0)

    gain_now = gain_start
    groups, pairs = local_sums(gain_now)
    pl.semaphore_wait(barrier, (nz - 1) + (nb - 1))
    all_reduce(0)
    gain_now = solve(gain_now, groups, pairs, 0)
    for r in range(1, rounds):
        local_sums(gain_now)
        all_reduce(r)
        gain_now = solve(gain_now, groups, pairs, r)
    o_ref[...] = gain_now
    final_model = model_rows(split_three(gain_now), coher_now, onehot_p, onehot_q)
    res_out[...] = jnp.concatenate([target[i] - final_model[i] for i in range(8)], 0)


def matmul_rows(left, right):
    pieces = []
    for i in (0, 1):
        for j in (0, 1):
            left_r0, left_i0 = left[4 * i], left[4 * i + 1]
            left_r1, left_i1 = left[4 * i + 2], left[4 * i + 3]
            right_r0, right_i0 = right[2 * j], right[2 * j + 1]
            right_r1, right_i1 = right[4 + 2 * j], right[4 + 2 * j + 1]
            pieces.append(
                left_r0 * right_r0 - left_i0 * right_i0 + left_r1 * right_r1 - left_i1 * right_i1
            )
            pieces.append(
                left_r0 * right_i0 + left_i0 * right_r0 + left_r1 * right_i1 + left_i1 * right_r1
            )
    return pieces


def adjoint_rows(mat):
    return [mat[0], -mat[1], mat[4], -mat[5], mat[2], -mat[3], mat[6], -mat[7]]


def gram_rows(gram):
    return [gram[0], gram[6], gram[2], gram[3]]


def damped_rounds(
    rounds, which, damp_value, gain_table, residual, coher_all, onehot_p, onehot_q, nb, nz
):
    stations = gain_table.shape[2]
    per = (16 * stations) // (nb * 2 * 128)
    vmem = pl.BlockSpec(memory_space=pltpu.VMEM)
    smem = pl.BlockSpec(memory_space=pltpu.SMEM)
    return pl.pallas_call(
        functools.partial(round_kernel, nb, nz, rounds),
        out_shape=(
            jax.ShapeDtypeStruct(gain_table.shape[1:], gain_table.dtype),
            jax.ShapeDtypeStruct(residual.shape, residual.dtype),
        ),
        in_specs=[smem, smem] + [vmem] * 5,
        out_specs=(vmem, vmem),
        scratch_shapes=[
            pltpu.VMEM((nb, per, 2, 128), jnp.float32),
            pltpu.VMEM((rounds, nb, per, 2, 128), jnp.float32),
            pltpu.VMEM((rounds, nz, per, 2, 128), jnp.float32),
            pltpu.VMEM((rounds, nb, per, 2, 128), jnp.float32),
            pltpu.SemaphoreType.DMA((rounds, nb)),
            pltpu.SemaphoreType.DMA((rounds, nb)),
            pltpu.SemaphoreType.DMA((rounds, nz)),
            pltpu.SemaphoreType.DMA((rounds, nz)),
            pltpu.SemaphoreType.DMA((rounds, nb)),
            pltpu.SemaphoreType.DMA((rounds, nb)),
        ],
        compiler_params=pltpu.CompilerParams(collective_id=2 * rounds, has_side_effects=True),
    )(
        which.reshape(1), damp_value.reshape(1, 1), gain_table, residual, coher_all, onehot_p,
        onehot_q,
    )


def prologue_kernel(nb, nz, coh_ref, gain_ref, coh_out, gain_out, coh_buf, gain_buf, s1, q1, s2, q2):
    mz = lax.axis_index("dir")
    mb = lax.axis_index("bl")
    z_peers = [lax.rem(mz + k, nz) for k in range(1, nz)]
    b_peers = [lax.rem(mb + k, nb) for k in range(1, nb)]

    barrier = pltpu.get_barrier_semaphore()
    for p in b_peers:
        pl.semaphore_signal(barrier, 1, device_id=(p, mz), device_id_type=MESH_ID)
    for p in z_peers:
        pl.semaphore_signal(barrier, 1, device_id=(mb, p), device_id_type=MESH_ID)
    pl.semaphore_wait(barrier, (nz - 1) + (nb - 1))

    sent = []
    for p in z_peers:
        c = pltpu.make_async_remote_copy(
            src_ref=coh_ref.at[p],
            dst_ref=coh_buf.at[mz],
            send_sem=s1.at[p],
            recv_sem=q1.at[mz],
            device_id=(mb, p),
            device_id_type=MESH_ID,
        )
        c.start()
        sent.append(c)
    for p in b_peers:
        c = pltpu.make_async_remote_copy(
            src_ref=gain_ref,
            dst_ref=gain_buf.at[mb],
            send_sem=s2.at[p],
            recv_sem=q2.at[mb],
            device_id=(p, mz),
            device_id_type=MESH_ID,
        )
        c.start()
        sent.append(c)
    coh_buf[mz] = coh_ref[mz]
    gain_buf[mb] = gain_ref[...]
    for p in z_peers:
        pltpu.make_async_remote_copy(
            src_ref=coh_buf.at[p],
            dst_ref=coh_buf.at[p],
            send_sem=s1.at[p],
            recv_sem=q1.at[p],
            device_id=(mb, p),
            device_id_type=MESH_ID,
        ).wait_recv()
    for p in b_peers:
        pltpu.make_async_remote_copy(
            src_ref=gain_buf.at[p],
            dst_ref=gain_buf.at[p],
            send_sem=s2.at[p],
            recv_sem=q2.at[p],
            device_id=(p, mz),
            device_id_type=MESH_ID,
        ).wait_recv()
    for c in sent:
        c.wait_send()
    coh_out[...] = coh_buf[...]
    gain_out[...] = gain_buf[...]


def exchange_inputs(coh_by_channel, gain_block, nb, nz):
    vmem = pl.BlockSpec(memory_space=pltpu.VMEM)
    coh_shape = (nz,) + coh_by_channel.shape[1:]
    gain_shape = (nb,) + gain_block.shape
    return pl.pallas_call(
        functools.partial(prologue_kernel, nb, nz),
        out_shape=(
            jax.ShapeDtypeStruct(coh_shape, coh_by_channel.dtype),
            jax.ShapeDtypeStruct(gain_shape, gain_block.dtype),
        ),
        in_specs=[vmem, vmem],
        out_specs=(vmem, vmem),
        scratch_shapes=[
            pltpu.VMEM(coh_shape, coh_by_channel.dtype),
            pltpu.VMEM(gain_shape, gain_block.dtype),
            pltpu.SemaphoreType.DMA((nz,)),
            pltpu.SemaphoreType.DMA((nz,)),
            pltpu.SemaphoreType.DMA((nb,)),
            pltpu.SemaphoreType.DMA((nb,)),
        ],
        compiler_params=pltpu.CompilerParams(collective_id=1, has_side_effects=True),
    )(coh_by_channel, gain_block)


def on_device(visibilities, coherencies, gain_offsets, stations, solve_order, counts, damping):
    identity = jnp.zeros((8,), jnp.float32).at[0].set(1.0).at[6].set(1.0)
    groups = lax.axis_size("bl")
    nz = lax.axis_size("dir")
    owned, _, channels_all, width = coherencies.shape
    by_channel = jnp.transpose(coherencies, (2, 0, 1, 3)).reshape(channels_all, owned * 8, width)
    coh_recv, gain_recv = exchange_inputs(
        by_channel, gain_offsets.reshape(-1, 128), groups, nz
    )
    direction_total = gain_offsets.shape[0]
    offsets = jnp.transpose(
        gain_recv.reshape((groups,) + gain_offsets.shape), (1, 2, 0, 3)
    ).reshape(direction_total, 8, groups * gain_offsets.shape[2])
    start = offsets + identity[None, :, None]
    coher_all = coh_recv.reshape(nz * owned, 8, 1, width)
    total_channels = coherencies.shape[2]
    station_count = start.shape[2]
    damping_factor = visibilities.shape[2] * groups * total_channels / station_count
    ends_p = jnp.take(start, stations[0], axis=2)
    ends_q = jnp.take(start, stations[1], axis=2)
    gain_p = jnp.transpose(ends_p, (1, 0, 2))[:, :, None, :]
    gain_q = jnp.transpose(ends_q, (1, 0, 2))[:, :, None, :]
    coher_f32 = jnp.transpose(coher_all, (1, 0, 2, 3)).astype(jnp.float32)
    first_model = jnp.sum(apply_gains(gain_p, coher_f32, gain_q), axis=1)
    first_residual = visibilities - first_model

    station_ids = lax.broadcasted_iota(jnp.int32, (station_count, stations.shape[1]), 0)
    onehot_p = (station_ids == stations[0][None, :]).astype(jnp.bfloat16)
    onehot_q = (station_ids == stations[1][None, :]).astype(jnp.bfloat16)

    def direction_model(gain_now, coher_now):
        gain_p = jnp.take(gain_now, stations[0], axis=1)[:, None, :]
        gain_q = jnp.take(gain_now, stations[1], axis=1)[:, None, :]
        return apply_gains(gain_p, coher_now, gain_q)

    coher_rows = coher_all.reshape(coher_all.shape[0], 8, coher_all.shape[3])

    def sweep(step_index, state):
        gain_table, residual = state
        which = solve_order[step_index]
        damp_value = damping[which].astype(jnp.float32) * damping_factor
        residual_before = residual[:, 0, :]

        def run(rounds):
            def branch(operands):
                if rounds == 0:
                    return (gain_table[which], residual_before)
                return damped_rounds(
                    rounds, which, damp_value, gain_table, residual_before, coher_rows,
                    onehot_p, onehot_q, groups, nz,
                )

            return branch

        rounds = jnp.clip(counts[which], 0, LM_ITERS)
        gain_final, residual_after = lax.switch(
            rounds, [run(r) for r in range(LM_ITERS + 1)], None
        )
        return (gain_table.at[which].set(gain_final), residual_after[:, None, :])

    gain_table, residual = lax.fori_loop(0, SOLVED, sweep, (start, first_residual))
    own_width = station_count // groups
    gains = lax.dynamic_slice_in_dim(gain_table, lax.axis_index("bl") * own_width, own_width, 2)
    return (gains, residual)


def solution(mesh):
    return jax.shard_map(
        on_device,
        mesh=mesh,
        in_specs=(
            P(None, "dir", "bl"),
            P("dir", None, None, "bl"),
            P(None, None, "bl"),
            P(None, "bl"),
            P(),
            P(),
            P(),
        ),
        out_specs=(P(None, None, "bl"), P(None, "dir", "bl")),
        check_vma=False,
    )
```

```python
import functools

import jax
import jax.numpy as jnp
from jax import lax
from jax.sharding import PartitionSpec as P
from jax.experimental import pallas as pl
from jax.experimental.pallas import tpu as pltpu

MESH_ID = pl.DeviceIdType.MESH

LM_ITERS = 2
SOLVED = 4


def matrix_entry(mat, i, j):
    return (mat[4 * i + 2 * j], mat[4 * i + 2 * j + 1])


def matmul_two(left, right):
    pieces = []
    for i in (0, 1):
        for j in (0, 1):
            left_r0, left_i0 = matrix_entry(left, i, 0)
            left_r1, left_i1 = matrix_entry(left, i, 1)
            right_r0, right_i0 = matrix_entry(right, 0, j)
            right_r1, right_i1 = matrix_entry(right, 1, j)
            pieces.append(
                left_r0 * right_r0 - left_i0 * right_i0 + left_r1 * right_r1 - left_i1 * right_i1
            )
            pieces.append(
                left_r0 * right_i0 + left_i0 * right_r0 + left_r1 * right_i1 + left_i1 * right_r1
            )
    return jnp.stack(pieces)


def adjoint(mat):
    return jnp.stack([mat[0], -mat[1], mat[4], -mat[5], mat[2], -mat[3], mat[6], -mat[7]])


def apply_gains(gain_p, coher_now, gain_q):
    return matmul_two(matmul_two(gain_p, coher_now), adjoint(gain_q))


def gram_parts(gram):
    return jnp.stack([gram[0], gram[6], gram[2], gram[3]])


def station_terms(gain_p, gain_q, coher_now, target):
    z_rows = matmul_two(coher_now, adjoint(gain_q))
    y_rows = matmul_two(adjoint(coher_now), adjoint(gain_p))
    leading_endpoint = jnp.concatenate(
        [matmul_two(target, adjoint(z_rows)), gram_parts(matmul_two(z_rows, adjoint(z_rows)))], 0
    )
    second = jnp.concatenate(
        [
            matmul_two(adjoint(target), adjoint(y_rows)),
            gram_parts(matmul_two(y_rows, adjoint(y_rows))),
        ],
        0,
    )
    return (jnp.sum(leading_endpoint, axis=1), jnp.sum(second, axis=1))


def solve_station(gathered_sums, gain_now, damp_value):
    numerator = gathered_sums[:8] + damp_value * gain_now
    diag_a = gathered_sums[8] + damp_value
    diag_d = gathered_sums[9] + damp_value
    cross_r = gathered_sums[10]
    cross_i = gathered_sums[11]
    determinant = diag_a * diag_d - cross_r * cross_r - cross_i * cross_i
    zeros_row = jnp.zeros_like(determinant)
    inverse = (
        jnp.stack([diag_d, zeros_row, -cross_r, -cross_i, -cross_r, cross_i, diag_a, zeros_row])
        / determinant
    )
    return matmul_two(numerator, inverse)


def split_three(x):
    hi = x.astype(jnp.bfloat16)
    rest = x - hi.astype(jnp.float32)
    mid = rest.astype(jnp.bfloat16)
    lo = (rest - mid.astype(jnp.float32)).astype(jnp.bfloat16)
    return (hi, mid, lo)


def gather_cols(parts, onehot):
    out = None
    for part in parts:
        term = jnp.dot(part, onehot, preferred_element_type=jnp.float32)
        out = term if out is None else out + term
    return out


def scatter_cols(values, onehot):
    out = None
    for part in split_three(values):
        term = lax.dot_general(
            part, onehot, (((1,), (1,)), ((), ())), preferred_element_type=jnp.float32
        )
        out = term if out is None else out + term
    return out


def rows_of(x):
    return [x[i : i + 1, :] for i in range(x.shape[0])]


def model_rows(gain_parts, coher_now, onehot_p, onehot_q):
    gain_p = rows_of(gather_cols(gain_parts, onehot_p))
    gain_q = rows_of(gather_cols(gain_parts, onehot_q))
    return matmul_rows(matmul_rows(gain_p, coher_now), adjoint_rows(gain_q))


def round_kernel(
    nb, nz, rounds, which_ref, damp_ref, table_ref, residual_ref, coher_ref, onehot_p_ref,
    onehot_q_ref, table_out, res_out, pay, r1, r2, r3, s1, q1, s2, q2, s3, q3,
):
    mz = lax.axis_index("dir")
    mb = lax.axis_index("bl")
    z_peers = [lax.rem(mz + k, nz) for k in range(1, nz)]
    b_peers = [lax.rem(mb + k, nb) for k in range(1, nb)]

    barrier = pltpu.get_barrier_semaphore()
    for p in b_peers:
        pl.semaphore_signal(barrier, 1, device_id=(p, mz), device_id_type=MESH_ID)
    for p in z_peers:
        pl.semaphore_signal(barrier, 1, device_id=(mb, p), device_id_type=MESH_ID)

    which = which_ref[0]
    gain_start = table_ref[which]
    coher_now = rows_of(coher_ref[which].astype(jnp.float32))
    onehot_p = onehot_p_ref[...]
    onehot_q = onehot_q_ref[...]
    start_model = model_rows(split_three(gain_start), coher_now, onehot_p, onehot_q)
    residual_rows = rows_of(residual_ref[...])
    target = [residual_rows[i] + start_model[i] for i in range(8)]
    damp_value = damp_ref[0, 0]
    groups = None
    pairs = None
    per = pay.shape[1]

    def exchange(peers, src_of, buf, me, send_sems, recv_sems, device_of, r):
        sent = []
        for p in peers:
            c = pltpu.make_async_remote_copy(
                src_ref=src_of(p),
                dst_ref=buf.at[r, me],
                send_sem=send_sems.at[r, p],
                recv_sem=recv_sems.at[r, me],
                device_id=device_of(p),
                device_id_type=MESH_ID,
            )
            c.start()
            sent.append(c)
        for p in peers:
            pltpu.make_async_remote_copy(
                src_ref=buf.at[r, p],
                dst_ref=buf.at[r, p],
                send_sem=send_sems.at[r, p],
                recv_sem=recv_sems.at[r, p],
                device_id=device_of(p),
                device_id_type=MESH_ID,
            ).wait_recv()
        for c in sent:
            c.wait_send()

    def local_sums(gain_now):
        parts = split_three(gain_now)
        gain_p = rows_of(gather_cols(parts, onehot_p))
        gain_q = rows_of(gather_cols(parts, onehot_q))
        z_rows = matmul_rows(coher_now, adjoint_rows(gain_q))
        y_rows = matmul_rows(adjoint_rows(coher_now), adjoint_rows(gain_p))
        zero_row = jnp.zeros_like(target[0])
        leading = (
            matmul_rows(target, adjoint_rows(z_rows))
            + gram_rows(matmul_rows(z_rows, adjoint_rows(z_rows)))
            + [zero_row] * 4
        )
        second = (
            matmul_rows(adjoint_rows(target), adjoint_rows(y_rows))
            + gram_rows(matmul_rows(y_rows, adjoint_rows(y_rows)))
            + [zero_row] * 4
        )
        sums = scatter_cols(jnp.concatenate(leading, 0), onehot_p) + scatter_cols(
            jnp.concatenate(second, 0), onehot_q
        )
        groups = sums.shape[1] // 128
        pairs = sums.shape[0] // 2
        for g in range(groups):
            for h in range(pairs):
                slab = g * pairs + h
                pay[slab // per, slab % per] = sums[2 * h : 2 * h + 2, 128 * g : 128 * g + 128]
        return groups, pairs

    def all_reduce(r):
        exchange(b_peers, lambda p: pay.at[p], r1, mb, s1, q1, lambda p: (p, mz), r)
        own = pay[mb]
        for p in b_peers:
            own = own + r1[r, p]
        r2[r, mz] = own
        exchange(z_peers, lambda p: r2.at[r, mz], r2, mz, s2, q2, lambda p: (mb, p), r)
        total = r2[r, mz]
        for p in z_peers:
            total = total + r2[r, p]
        r3[r, mb] = total
        exchange(b_peers, lambda p: r3.at[r, mb], r3, mb, s3, q3, lambda p: (p, mz), r)

    def solve(gain_now, groups, pairs, r):
        gathered = []
        for h in range(pairs):
            for t in range(2):
                pieces = []
                for g in range(groups):
                    slab = g * pairs + h
                    pieces.append(r3[r, slab // per, slab % per, t : t + 1, :])
                gathered.append(jnp.concatenate(pieces, 1))
        gain_rows = rows_of(gain_now)
        numerator = [gathered[i] + damp_value * gain_rows[i] for i in range(8)]
        diag_a = gathered[8] + damp_value
        diag_d = gathered[9] + damp_value
        cross_r = gathered[10]
        cross_i = gathered[11]
        determinant = diag_a * diag_d - cross_r * cross_r - cross_i * cross_i
        zeros_row = jnp.zeros_like(determinant)
        inverse = [
            v / determinant
            for v in (diag_d, zeros_row, -cross_r, -cross_i, -cross_r, cross_i, diag_a, zeros_row)
        ]
        return jnp.concatenate(matmul_rows(numerator, inverse), 0)

    gain_now = gain_start
    groups, pairs = local_sums(gain_now)
    pl.semaphore_wait(barrier, (nz - 1) + (nb - 1))
    all_reduce(0)
    gain_now = solve(gain_now, groups, pairs, 0)
    for r in range(1, rounds):
        local_sums(gain_now)
        all_reduce(r)
        gain_now = solve(gain_now, groups, pairs, r)
    for d in range(table_ref.shape[0]):
        table_out[d] = jnp.where(which == d, gain_now, table_ref[d])
    final_model = model_rows(split_three(gain_now), coher_now, onehot_p, onehot_q)
    res_out[...] = jnp.concatenate([target[i] - final_model[i] for i in range(8)], 0)


def matmul_rows(left, right):
    pieces = []
    for i in (0, 1):
        for j in (0, 1):
            left_r0, left_i0 = left[4 * i], left[4 * i + 1]
            left_r1, left_i1 = left[4 * i + 2], left[4 * i + 3]
            right_r0, right_i0 = right[2 * j], right[2 * j + 1]
            right_r1, right_i1 = right[4 + 2 * j], right[4 + 2 * j + 1]
            pieces.append(
                left_r0 * right_r0 - left_i0 * right_i0 + left_r1 * right_r1 - left_i1 * right_i1
            )
            pieces.append(
                left_r0 * right_i0 + left_i0 * right_r0 + left_r1 * right_i1 + left_i1 * right_r1
            )
    return pieces


def adjoint_rows(mat):
    return [mat[0], -mat[1], mat[4], -mat[5], mat[2], -mat[3], mat[6], -mat[7]]


def gram_rows(gram):
    return [gram[0], gram[6], gram[2], gram[3]]


def damped_rounds(
    rounds, which, damp_value, gain_table, residual, coher_all, onehot_p, onehot_q, nb, nz
):
    stations = gain_table.shape[2]
    per = (16 * stations) // (nb * 2 * 128)
    vmem = pl.BlockSpec(memory_space=pltpu.VMEM)
    smem = pl.BlockSpec(memory_space=pltpu.SMEM)
    return pl.pallas_call(
        functools.partial(round_kernel, nb, nz, rounds),
        out_shape=(
            jax.ShapeDtypeStruct(gain_table.shape, gain_table.dtype),
            jax.ShapeDtypeStruct(residual.shape, residual.dtype),
        ),
        in_specs=[smem, smem] + [vmem] * 5,
        out_specs=(vmem, vmem),
        scratch_shapes=[
            pltpu.VMEM((nb, per, 2, 128), jnp.float32),
            pltpu.VMEM((rounds, nb, per, 2, 128), jnp.float32),
            pltpu.VMEM((rounds, nz, per, 2, 128), jnp.float32),
            pltpu.VMEM((rounds, nb, per, 2, 128), jnp.float32),
            pltpu.SemaphoreType.DMA((rounds, nb)),
            pltpu.SemaphoreType.DMA((rounds, nb)),
            pltpu.SemaphoreType.DMA((rounds, nz)),
            pltpu.SemaphoreType.DMA((rounds, nz)),
            pltpu.SemaphoreType.DMA((rounds, nb)),
            pltpu.SemaphoreType.DMA((rounds, nb)),
        ],
        compiler_params=pltpu.CompilerParams(collective_id=2 * rounds, has_side_effects=True),
    )(
        which.reshape(1), damp_value.reshape(1, 1), gain_table, residual, coher_all, onehot_p,
        onehot_q,
    )


def prologue_kernel(nb, nz, coh_ref, gain_ref, coh_out, gain_out, coh_buf, gain_buf, s1, q1, s2, q2):
    mz = lax.axis_index("dir")
    mb = lax.axis_index("bl")
    z_peers = [lax.rem(mz + k, nz) for k in range(1, nz)]
    b_peers = [lax.rem(mb + k, nb) for k in range(1, nb)]

    barrier = pltpu.get_barrier_semaphore()
    for p in b_peers:
        pl.semaphore_signal(barrier, 1, device_id=(p, mz), device_id_type=MESH_ID)
    for p in z_peers:
        pl.semaphore_signal(barrier, 1, device_id=(mb, p), device_id_type=MESH_ID)
    pl.semaphore_wait(barrier, (nz - 1) + (nb - 1))

    sent = []
    for p in z_peers:
        c = pltpu.make_async_remote_copy(
            src_ref=coh_ref.at[p],
            dst_ref=coh_buf.at[mz],
            send_sem=s1.at[p],
            recv_sem=q1.at[mz],
            device_id=(mb, p),
            device_id_type=MESH_ID,
        )
        c.start()
        sent.append(c)
    for p in b_peers:
        c = pltpu.make_async_remote_copy(
            src_ref=gain_ref,
            dst_ref=gain_buf.at[mb],
            send_sem=s2.at[p],
            recv_sem=q2.at[mb],
            device_id=(p, mz),
            device_id_type=MESH_ID,
        )
        c.start()
        sent.append(c)
    coh_buf[mz] = coh_ref[mz]
    gain_buf[mb] = gain_ref[...]
    for p in z_peers:
        pltpu.make_async_remote_copy(
            src_ref=coh_buf.at[p],
            dst_ref=coh_buf.at[p],
            send_sem=s1.at[p],
            recv_sem=q1.at[p],
            device_id=(mb, p),
            device_id_type=MESH_ID,
        ).wait_recv()
    for p in b_peers:
        pltpu.make_async_remote_copy(
            src_ref=gain_buf.at[p],
            dst_ref=gain_buf.at[p],
            send_sem=s2.at[p],
            recv_sem=q2.at[p],
            device_id=(p, mz),
            device_id_type=MESH_ID,
        ).wait_recv()
    for c in sent:
        c.wait_send()
    coh_out[...] = coh_buf[...]
    gain_out[...] = gain_buf[...]


def exchange_inputs(coh_by_channel, gain_block, nb, nz):
    vmem = pl.BlockSpec(memory_space=pltpu.VMEM)
    coh_shape = (nz,) + coh_by_channel.shape[1:]
    gain_shape = (nb,) + gain_block.shape
    return pl.pallas_call(
        functools.partial(prologue_kernel, nb, nz),
        out_shape=(
            jax.ShapeDtypeStruct(coh_shape, coh_by_channel.dtype),
            jax.ShapeDtypeStruct(gain_shape, gain_block.dtype),
        ),
        in_specs=[vmem, vmem],
        out_specs=(vmem, vmem),
        scratch_shapes=[
            pltpu.VMEM(coh_shape, coh_by_channel.dtype),
            pltpu.VMEM(gain_shape, gain_block.dtype),
            pltpu.SemaphoreType.DMA((nz,)),
            pltpu.SemaphoreType.DMA((nz,)),
            pltpu.SemaphoreType.DMA((nb,)),
            pltpu.SemaphoreType.DMA((nb,)),
        ],
        compiler_params=pltpu.CompilerParams(collective_id=1, has_side_effects=True),
    )(coh_by_channel, gain_block)


def on_device(visibilities, coherencies, gain_offsets, stations, solve_order, counts, damping):
    identity = jnp.zeros((8,), jnp.float32).at[0].set(1.0).at[6].set(1.0)
    groups = lax.axis_size("bl")
    nz = lax.axis_size("dir")
    owned, _, channels_all, width = coherencies.shape
    by_channel = jnp.transpose(coherencies, (2, 0, 1, 3)).reshape(channels_all, owned * 8, width)
    coh_recv, gain_recv = exchange_inputs(
        by_channel, gain_offsets.reshape(-1, 128), groups, nz
    )
    direction_total = gain_offsets.shape[0]
    offsets = jnp.transpose(
        gain_recv.reshape((groups,) + gain_offsets.shape), (1, 2, 0, 3)
    ).reshape(direction_total, 8, groups * gain_offsets.shape[2])
    start = offsets + identity[None, :, None]
    coher_all = coh_recv.reshape(nz * owned, 8, 1, width)
    total_channels = coherencies.shape[2]
    station_count = start.shape[2]
    damping_factor = visibilities.shape[2] * groups * total_channels / station_count
    ends_p = jnp.take(start, stations[0], axis=2)
    ends_q = jnp.take(start, stations[1], axis=2)
    gain_p = jnp.transpose(ends_p, (1, 0, 2))[:, :, None, :]
    gain_q = jnp.transpose(ends_q, (1, 0, 2))[:, :, None, :]
    coher_f32 = jnp.transpose(coher_all, (1, 0, 2, 3)).astype(jnp.float32)
    first_model = jnp.sum(apply_gains(gain_p, coher_f32, gain_q), axis=1)
    first_residual = visibilities - first_model

    station_ids = lax.broadcasted_iota(jnp.int32, (station_count, stations.shape[1]), 0)
    onehot_p = (station_ids == stations[0][None, :]).astype(jnp.bfloat16)
    onehot_q = (station_ids == stations[1][None, :]).astype(jnp.bfloat16)

    def direction_model(gain_now, coher_now):
        gain_p = jnp.take(gain_now, stations[0], axis=1)[:, None, :]
        gain_q = jnp.take(gain_now, stations[1], axis=1)[:, None, :]
        return apply_gains(gain_p, coher_now, gain_q)

    coher_rows = coher_all.reshape(coher_all.shape[0], 8, coher_all.shape[3])

    def sweep(step_index, state):
        gain_table, residual = state
        which = solve_order[step_index]
        damp_value = damping[which].astype(jnp.float32) * damping_factor

        def run(rounds):
            def branch(operands):
                if rounds == 0:
                    return (gain_table, residual)
                return damped_rounds(
                    rounds, which, damp_value, gain_table, residual, coher_rows,
                    onehot_p, onehot_q, groups, nz,
                )

            return branch

        rounds = jnp.clip(counts[which], 0, LM_ITERS)
        return lax.switch(rounds, [run(r) for r in range(LM_ITERS + 1)], None)

    gain_table, residual_rows = lax.fori_loop(
        0, SOLVED, sweep, (start, first_residual[:, 0, :])
    )
    residual = residual_rows[:, None, :]
    own_width = station_count // groups
    gains = lax.dynamic_slice_in_dim(gain_table, lax.axis_index("bl") * own_width, own_width, 2)
    return (gains, residual)


def solution(mesh):
    return jax.shard_map(
        on_device,
        mesh=mesh,
        in_specs=(
            P(None, "dir", "bl"),
            P("dir", None, None, "bl"),
            P(None, None, "bl"),
            P(None, "bl"),
            P(),
            P(),
            P(),
        ),
        out_specs=(P(None, None, "bl"), P(None, "dir", "bl")),
        check_vma=False,
    )
```

```python
import functools

import jax
import jax.numpy as jnp
from jax import lax
from jax.sharding import PartitionSpec as P
from jax.experimental import pallas as pl
from jax.experimental.pallas import tpu as pltpu

MESH_ID = pl.DeviceIdType.MESH

LM_ITERS = 2
SOLVED = 4


def matrix_entry(mat, i, j):
    return (mat[4 * i + 2 * j], mat[4 * i + 2 * j + 1])


def matmul_two(left, right):
    pieces = []
    for i in (0, 1):
        for j in (0, 1):
            left_r0, left_i0 = matrix_entry(left, i, 0)
            left_r1, left_i1 = matrix_entry(left, i, 1)
            right_r0, right_i0 = matrix_entry(right, 0, j)
            right_r1, right_i1 = matrix_entry(right, 1, j)
            pieces.append(
                left_r0 * right_r0 - left_i0 * right_i0 + left_r1 * right_r1 - left_i1 * right_i1
            )
            pieces.append(
                left_r0 * right_i0 + left_i0 * right_r0 + left_r1 * right_i1 + left_i1 * right_r1
            )
    return jnp.stack(pieces)


def adjoint(mat):
    return jnp.stack([mat[0], -mat[1], mat[4], -mat[5], mat[2], -mat[3], mat[6], -mat[7]])


def apply_gains(gain_p, coher_now, gain_q):
    return matmul_two(matmul_two(gain_p, coher_now), adjoint(gain_q))


def gram_parts(gram):
    return jnp.stack([gram[0], gram[6], gram[2], gram[3]])


def station_terms(gain_p, gain_q, coher_now, target):
    z_rows = matmul_two(coher_now, adjoint(gain_q))
    y_rows = matmul_two(adjoint(coher_now), adjoint(gain_p))
    leading_endpoint = jnp.concatenate(
        [matmul_two(target, adjoint(z_rows)), gram_parts(matmul_two(z_rows, adjoint(z_rows)))], 0
    )
    second = jnp.concatenate(
        [
            matmul_two(adjoint(target), adjoint(y_rows)),
            gram_parts(matmul_two(y_rows, adjoint(y_rows))),
        ],
        0,
    )
    return (jnp.sum(leading_endpoint, axis=1), jnp.sum(second, axis=1))


def solve_station(gathered_sums, gain_now, damp_value):
    numerator = gathered_sums[:8] + damp_value * gain_now
    diag_a = gathered_sums[8] + damp_value
    diag_d = gathered_sums[9] + damp_value
    cross_r = gathered_sums[10]
    cross_i = gathered_sums[11]
    determinant = diag_a * diag_d - cross_r * cross_r - cross_i * cross_i
    zeros_row = jnp.zeros_like(determinant)
    inverse = (
        jnp.stack([diag_d, zeros_row, -cross_r, -cross_i, -cross_r, cross_i, diag_a, zeros_row])
        / determinant
    )
    return matmul_two(numerator, inverse)


def split_three(x):
    hi = x.astype(jnp.bfloat16)
    rest = x - hi.astype(jnp.float32)
    mid = rest.astype(jnp.bfloat16)
    lo = (rest - mid.astype(jnp.float32)).astype(jnp.bfloat16)
    return (hi, mid, lo)


def gather_cols(parts, onehot):
    out = None
    for part in parts:
        term = jnp.dot(part, onehot, preferred_element_type=jnp.float32)
        out = term if out is None else out + term
    return out


def scatter_cols(values, onehot):
    out = None
    for part in split_three(values):
        term = lax.dot_general(
            part, onehot, (((1,), (1,)), ((), ())), preferred_element_type=jnp.float32
        )
        out = term if out is None else out + term
    return out


def rows_of(x):
    return [x[i : i + 1, :] for i in range(x.shape[0])]


def model_rows(gain_parts, coher_now, onehot_p, onehot_q):
    gain_p = rows_of(gather_cols(gain_parts, onehot_p))
    gain_q = rows_of(gather_cols(gain_parts, onehot_q))
    return matmul_rows(matmul_rows(gain_p, coher_now), adjoint_rows(gain_q))


def round_kernel(
    nb, nz, rounds, which_ref, damp_ref, table_ref, residual_ref, coher_ref, onehot_p_ref,
    onehot_q_ref, table_out, res_out, pay, r1, r2, r3, s1, q1, s2, q2, s3, q3,
):
    mz = lax.axis_index("dir")
    mb = lax.axis_index("bl")
    z_peers = [lax.rem(mz + k, nz) for k in range(1, nz)]
    b_peers = [lax.rem(mb + k, nb) for k in range(1, nb)]

    barrier = pltpu.get_barrier_semaphore()
    for p in b_peers:
        pl.semaphore_signal(barrier, 1, device_id=(p, mz), device_id_type=MESH_ID)
    for p in z_peers:
        pl.semaphore_signal(barrier, 1, device_id=(mb, p), device_id_type=MESH_ID)

    which = which_ref[0]
    gain_start = table_ref[which]
    coher_now = rows_of(coher_ref[which].astype(jnp.float32))
    onehot_p = onehot_p_ref[...]
    onehot_q = onehot_q_ref[...]
    start_model = model_rows(split_three(gain_start), coher_now, onehot_p, onehot_q)
    residual_rows = rows_of(residual_ref[...])
    target = [residual_rows[i] + start_model[i] for i in range(8)]
    damp_value = damp_ref[0, 0]
    groups = None
    pairs = None
    per = pay.shape[1]

    def exchange(peers, src_of, buf, me, send_sems, recv_sems, device_of, r):
        sent = []
        for p in peers:
            c = pltpu.make_async_remote_copy(
                src_ref=src_of(p),
                dst_ref=buf.at[r, me],
                send_sem=send_sems.at[r, p],
                recv_sem=recv_sems.at[r, me],
                device_id=device_of(p),
                device_id_type=MESH_ID,
            )
            c.start()
            sent.append(c)
        for p in peers:
            pltpu.make_async_remote_copy(
                src_ref=buf.at[r, p],
                dst_ref=buf.at[r, p],
                send_sem=send_sems.at[r, p],
                recv_sem=recv_sems.at[r, p],
                device_id=device_of(p),
                device_id_type=MESH_ID,
            ).wait_recv()
        for c in sent:
            c.wait_send()

    def local_sums(gain_now):
        parts = split_three(gain_now)
        gain_p = rows_of(gather_cols(parts, onehot_p))
        gain_q = rows_of(gather_cols(parts, onehot_q))
        z_rows = matmul_rows(coher_now, adjoint_rows(gain_q))
        y_rows = matmul_rows(adjoint_rows(coher_now), adjoint_rows(gain_p))
        zero_row = jnp.zeros_like(target[0])
        leading = (
            matmul_rows(target, adjoint_rows(z_rows))
            + gram_rows(matmul_rows(z_rows, adjoint_rows(z_rows)))
            + [zero_row] * 4
        )
        second = (
            matmul_rows(adjoint_rows(target), adjoint_rows(y_rows))
            + gram_rows(matmul_rows(y_rows, adjoint_rows(y_rows)))
            + [zero_row] * 4
        )
        sums = scatter_cols(jnp.concatenate(leading, 0), onehot_p) + scatter_cols(
            jnp.concatenate(second, 0), onehot_q
        )
        groups = sums.shape[1] // 128
        pairs = sums.shape[0] // 2
        for g in range(groups):
            for h in range(pairs):
                slab = g * pairs + h
                pay[slab // per, slab % per] = sums[2 * h : 2 * h + 2, 128 * g : 128 * g + 128]
        return groups, pairs

    def all_reduce(r):
        exchange(b_peers, lambda p: pay.at[p], r1, mb, s1, q1, lambda p: (p, mz), r)
        own = pay[mb]
        for p in b_peers:
            own = own + r1[r, p]
        r2[r, mz] = own
        exchange(z_peers, lambda p: r2.at[r, mz], r2, mz, s2, q2, lambda p: (mb, p), r)
        total = r2[r, mz]
        for p in z_peers:
            total = total + r2[r, p]
        r3[r, mb] = total
        exchange(b_peers, lambda p: r3.at[r, mb], r3, mb, s3, q3, lambda p: (p, mz), r)

    def solve(gain_now, groups, pairs, r):
        gathered = []
        for h in range(pairs):
            for t in range(2):
                pieces = []
                for g in range(groups):
                    slab = g * pairs + h
                    pieces.append(r3[r, slab // per, slab % per, t : t + 1, :])
                gathered.append(jnp.concatenate(pieces, 1))
        gain_rows = rows_of(gain_now)
        numerator = [gathered[i] + damp_value * gain_rows[i] for i in range(8)]
        diag_a = gathered[8] + damp_value
        diag_d = gathered[9] + damp_value
        cross_r = gathered[10]
        cross_i = gathered[11]
        determinant = diag_a * diag_d - cross_r * cross_r - cross_i * cross_i
        zeros_row = jnp.zeros_like(determinant)
        inverse = [
            v / determinant
            for v in (diag_d, zeros_row, -cross_r, -cross_i, -cross_r, cross_i, diag_a, zeros_row)
        ]
        return jnp.concatenate(matmul_rows(numerator, inverse), 0)

    gain_now = gain_start
    groups, pairs = local_sums(gain_now)
    pl.semaphore_wait(barrier, (nz - 1) + (nb - 1))
    all_reduce(0)
    gain_now = solve(gain_now, groups, pairs, 0)
    for r in range(1, rounds):
        local_sums(gain_now)
        all_reduce(r)
        gain_now = solve(gain_now, groups, pairs, r)
    for d in range(table_ref.shape[0]):
        table_out[d] = jnp.where(which == d, gain_now, table_ref[d])
    final_model = model_rows(split_three(gain_now), coher_now, onehot_p, onehot_q)
    res_out[...] = jnp.concatenate([target[i] - final_model[i] for i in range(8)], 0)


def matmul_rows(left, right):
    pieces = []
    for i in (0, 1):
        for j in (0, 1):
            left_r0, left_i0 = left[4 * i], left[4 * i + 1]
            left_r1, left_i1 = left[4 * i + 2], left[4 * i + 3]
            right_r0, right_i0 = right[2 * j], right[2 * j + 1]
            right_r1, right_i1 = right[4 + 2 * j], right[4 + 2 * j + 1]
            pieces.append(
                left_r0 * right_r0 - left_i0 * right_i0 + left_r1 * right_r1 - left_i1 * right_i1
            )
            pieces.append(
                left_r0 * right_i0 + left_i0 * right_r0 + left_r1 * right_i1 + left_i1 * right_r1
            )
    return pieces


def adjoint_rows(mat):
    return [mat[0], -mat[1], mat[4], -mat[5], mat[2], -mat[3], mat[6], -mat[7]]


def gram_rows(gram):
    return [gram[0], gram[6], gram[2], gram[3]]


def damped_rounds(
    rounds, which, damp_value, gain_table, residual, coher_all, onehot_p, onehot_q, nb, nz
):
    stations = gain_table.shape[2]
    per = (16 * stations) // (nb * 2 * 128)
    vmem = pl.BlockSpec(memory_space=pltpu.VMEM)
    smem = pl.BlockSpec(memory_space=pltpu.SMEM)
    return pl.pallas_call(
        functools.partial(round_kernel, nb, nz, rounds),
        out_shape=(
            jax.ShapeDtypeStruct(gain_table.shape, gain_table.dtype),
            jax.ShapeDtypeStruct(residual.shape, residual.dtype),
        ),
        in_specs=[smem, smem] + [vmem] * 5,
        out_specs=(vmem, vmem),
        scratch_shapes=[
            pltpu.VMEM((nb, per, 2, 128), jnp.float32),
            pltpu.VMEM((rounds, nb, per, 2, 128), jnp.float32),
            pltpu.VMEM((rounds, nz, per, 2, 128), jnp.float32),
            pltpu.VMEM((rounds, nb, per, 2, 128), jnp.float32),
            pltpu.SemaphoreType.DMA((rounds, nb)),
            pltpu.SemaphoreType.DMA((rounds, nb)),
            pltpu.SemaphoreType.DMA((rounds, nz)),
            pltpu.SemaphoreType.DMA((rounds, nz)),
            pltpu.SemaphoreType.DMA((rounds, nb)),
            pltpu.SemaphoreType.DMA((rounds, nb)),
        ],
        compiler_params=pltpu.CompilerParams(collective_id=2 * rounds, has_side_effects=True),
    )(
        which.reshape(1), damp_value.reshape(1, 1), gain_table, residual, coher_all, onehot_p,
        onehot_q,
    )


def prologue_kernel(nb, nz, coh_ref, gain_ref, coh_out, gain_out, coh_buf, gain_buf, s1, q1, s2, q2):
    mz = lax.axis_index("dir")
    mb = lax.axis_index("bl")
    z_peers = [lax.rem(mz + k, nz) for k in range(1, nz)]
    b_peers = [lax.rem(mb + k, nb) for k in range(1, nb)]

    barrier = pltpu.get_barrier_semaphore()
    for p in b_peers:
        pl.semaphore_signal(barrier, 1, device_id=(p, mz), device_id_type=MESH_ID)
    for p in z_peers:
        pl.semaphore_signal(barrier, 1, device_id=(mb, p), device_id_type=MESH_ID)
    pl.semaphore_wait(barrier, (nz - 1) + (nb - 1))

    sent = []
    for p in z_peers:
        c = pltpu.make_async_remote_copy(
            src_ref=coh_ref.at[p],
            dst_ref=coh_buf.at[mz],
            send_sem=s1.at[p],
            recv_sem=q1.at[mz],
            device_id=(mb, p),
            device_id_type=MESH_ID,
        )
        c.start()
        sent.append(c)
    for p in b_peers:
        c = pltpu.make_async_remote_copy(
            src_ref=gain_ref,
            dst_ref=gain_buf.at[mb],
            send_sem=s2.at[p],
            recv_sem=q2.at[mb],
            device_id=(p, mz),
            device_id_type=MESH_ID,
        )
        c.start()
        sent.append(c)
    coh_buf[mz] = coh_ref[mz]
    gain_buf[mb] = gain_ref[...]
    for p in z_peers:
        pltpu.make_async_remote_copy(
            src_ref=coh_buf.at[p],
            dst_ref=coh_buf.at[p],
            send_sem=s1.at[p],
            recv_sem=q1.at[p],
            device_id=(mb, p),
            device_id_type=MESH_ID,
        ).wait_recv()
    for p in b_peers:
        pltpu.make_async_remote_copy(
            src_ref=gain_buf.at[p],
            dst_ref=gain_buf.at[p],
            send_sem=s2.at[p],
            recv_sem=q2.at[p],
            device_id=(p, mz),
            device_id_type=MESH_ID,
        ).wait_recv()
    for c in sent:
        c.wait_send()
    coh_out[...] = coh_buf[...]
    gain_out[...] = gain_buf[...]


def exchange_inputs(coh_by_channel, gain_block, nb, nz):
    vmem = pl.BlockSpec(memory_space=pltpu.VMEM)
    coh_shape = (nz,) + coh_by_channel.shape[1:]
    gain_shape = (nb,) + gain_block.shape
    return pl.pallas_call(
        functools.partial(prologue_kernel, nb, nz),
        out_shape=(
            jax.ShapeDtypeStruct(coh_shape, coh_by_channel.dtype),
            jax.ShapeDtypeStruct(gain_shape, gain_block.dtype),
        ),
        in_specs=[vmem, vmem],
        out_specs=(vmem, vmem),
        scratch_shapes=[
            pltpu.VMEM(coh_shape, coh_by_channel.dtype),
            pltpu.VMEM(gain_shape, gain_block.dtype),
            pltpu.SemaphoreType.DMA((nz,)),
            pltpu.SemaphoreType.DMA((nz,)),
            pltpu.SemaphoreType.DMA((nb,)),
            pltpu.SemaphoreType.DMA((nb,)),
        ],
        compiler_params=pltpu.CompilerParams(collective_id=1, has_side_effects=True),
    )(coh_by_channel, gain_block)


def on_device(visibilities, coherencies, gain_offsets, stations, solve_order, counts, damping):
    identity = jnp.zeros((8,), jnp.float32).at[0].set(1.0).at[6].set(1.0)
    groups = lax.axis_size("bl")
    nz = lax.axis_size("dir")
    owned, _, channels_all, width = coherencies.shape
    by_channel = jnp.transpose(coherencies, (2, 0, 1, 3)).reshape(channels_all, owned * 8, width)
    coh_recv, gain_recv = exchange_inputs(
        by_channel, gain_offsets.reshape(-1, 128), groups, nz
    )
    direction_total = gain_offsets.shape[0]
    offsets = jnp.transpose(
        gain_recv.reshape((groups,) + gain_offsets.shape), (1, 2, 0, 3)
    ).reshape(direction_total, 8, groups * gain_offsets.shape[2])
    start = offsets + identity[None, :, None]
    coher_all = coh_recv.reshape(nz * owned, 8, 1, width)
    total_channels = coherencies.shape[2]
    station_count = start.shape[2]
    damping_factor = visibilities.shape[2] * groups * total_channels / station_count
    start_by_entry = jnp.transpose(start, (1, 0, 2))
    gain_p = jnp.take(start_by_entry, stations[0], axis=2)[:, :, None, :]
    gain_q = jnp.take(start_by_entry, stations[1], axis=2)[:, :, None, :]
    coher_f32 = jnp.transpose(coher_all, (1, 0, 2, 3)).astype(jnp.float32)
    first_model = jnp.sum(apply_gains(gain_p, coher_f32, gain_q), axis=1)
    first_residual = visibilities - first_model

    station_ids = lax.broadcasted_iota(jnp.int32, (station_count, stations.shape[1]), 0)
    onehot_p = (station_ids == stations[0][None, :]).astype(jnp.bfloat16)
    onehot_q = (station_ids == stations[1][None, :]).astype(jnp.bfloat16)

    def direction_model(gain_now, coher_now):
        gain_p = jnp.take(gain_now, stations[0], axis=1)[:, None, :]
        gain_q = jnp.take(gain_now, stations[1], axis=1)[:, None, :]
        return apply_gains(gain_p, coher_now, gain_q)

    coher_rows = coher_all.reshape(coher_all.shape[0], 8, coher_all.shape[3])

    def sweep(step_index, state):
        gain_table, residual = state
        which = solve_order[step_index]
        damp_value = damping[which].astype(jnp.float32) * damping_factor

        def run(rounds):
            def branch(operands):
                if rounds == 0:
                    return (gain_table, residual)
                return damped_rounds(
                    rounds, which, damp_value, gain_table, residual, coher_rows,
                    onehot_p, onehot_q, groups, nz,
                )

            return branch

        rounds = jnp.clip(counts[which], 0, LM_ITERS)
        return lax.switch(rounds, [run(r) for r in range(LM_ITERS + 1)], None)

    gain_table, residual_rows = lax.fori_loop(
        0, SOLVED, sweep, (start, first_residual[:, 0, :])
    )
    residual = residual_rows[:, None, :]
    own_width = station_count // groups
    gains = lax.dynamic_slice_in_dim(gain_table, lax.axis_index("bl") * own_width, own_width, 2)
    return (gains, residual)


def solution(mesh):
    return jax.shard_map(
        on_device,
        mesh=mesh,
        in_specs=(
            P(None, "dir", "bl"),
            P("dir", None, None, "bl"),
            P(None, None, "bl"),
            P(None, "bl"),
            P(),
            P(),
            P(),
        ),
        out_specs=(P(None, None, "bl"), P(None, "dir", "bl")),
        check_vma=False,
    )
```

```python
import functools

import jax
import jax.numpy as jnp
from jax import lax
from jax.sharding import PartitionSpec as P
from jax.experimental import pallas as pl
from jax.experimental.pallas import tpu as pltpu

MESH_ID = pl.DeviceIdType.MESH

LM_ITERS = 2
SOLVED = 4


def matrix_entry(mat, i, j):
    return (mat[4 * i + 2 * j], mat[4 * i + 2 * j + 1])


def matmul_two(left, right):
    pieces = []
    for i in (0, 1):
        for j in (0, 1):
            left_r0, left_i0 = matrix_entry(left, i, 0)
            left_r1, left_i1 = matrix_entry(left, i, 1)
            right_r0, right_i0 = matrix_entry(right, 0, j)
            right_r1, right_i1 = matrix_entry(right, 1, j)
            pieces.append(
                left_r0 * right_r0 - left_i0 * right_i0 + left_r1 * right_r1 - left_i1 * right_i1
            )
            pieces.append(
                left_r0 * right_i0 + left_i0 * right_r0 + left_r1 * right_i1 + left_i1 * right_r1
            )
    return jnp.stack(pieces)


def adjoint(mat):
    return jnp.stack([mat[0], -mat[1], mat[4], -mat[5], mat[2], -mat[3], mat[6], -mat[7]])


def apply_gains(gain_p, coher_now, gain_q):
    return matmul_two(matmul_two(gain_p, coher_now), adjoint(gain_q))


def gram_parts(gram):
    return jnp.stack([gram[0], gram[6], gram[2], gram[3]])


def station_terms(gain_p, gain_q, coher_now, target):
    z_rows = matmul_two(coher_now, adjoint(gain_q))
    y_rows = matmul_two(adjoint(coher_now), adjoint(gain_p))
    leading_endpoint = jnp.concatenate(
        [matmul_two(target, adjoint(z_rows)), gram_parts(matmul_two(z_rows, adjoint(z_rows)))], 0
    )
    second = jnp.concatenate(
        [
            matmul_two(adjoint(target), adjoint(y_rows)),
            gram_parts(matmul_two(y_rows, adjoint(y_rows))),
        ],
        0,
    )
    return (jnp.sum(leading_endpoint, axis=1), jnp.sum(second, axis=1))


def solve_station(gathered_sums, gain_now, damp_value):
    numerator = gathered_sums[:8] + damp_value * gain_now
    diag_a = gathered_sums[8] + damp_value
    diag_d = gathered_sums[9] + damp_value
    cross_r = gathered_sums[10]
    cross_i = gathered_sums[11]
    determinant = diag_a * diag_d - cross_r * cross_r - cross_i * cross_i
    zeros_row = jnp.zeros_like(determinant)
    inverse = (
        jnp.stack([diag_d, zeros_row, -cross_r, -cross_i, -cross_r, cross_i, diag_a, zeros_row])
        / determinant
    )
    return matmul_two(numerator, inverse)


def split_three(x):
    hi = x.astype(jnp.bfloat16)
    rest = x - hi.astype(jnp.float32)
    mid = rest.astype(jnp.bfloat16)
    lo = (rest - mid.astype(jnp.float32)).astype(jnp.bfloat16)
    return (hi, mid, lo)


def gather_cols(parts, onehot):
    out = None
    for part in parts:
        term = jnp.dot(part, onehot, preferred_element_type=jnp.float32)
        out = term if out is None else out + term
    return out


def scatter_cols(values, onehot):
    out = None
    for part in split_three(values):
        term = lax.dot_general(
            part, onehot, (((1,), (1,)), ((), ())), preferred_element_type=jnp.float32
        )
        out = term if out is None else out + term
    return out


def rows_of(x):
    return [x[i : i + 1, :] for i in range(x.shape[0])]


def model_rows(gain_parts, coher_now, onehot_p, onehot_q):
    gain_p = rows_of(gather_cols(gain_parts, onehot_p))
    gain_q = rows_of(gather_cols(gain_parts, onehot_q))
    return matmul_rows(matmul_rows(gain_p, coher_now), adjoint_rows(gain_q))


def round_kernel(
    nb, nz, rounds, which_ref, damp_ref, table_ref, residual_ref, coher_ref, onehot_p_ref,
    onehot_q_ref, table_out, res_out, pay, r1, r2, r3, s1, q1, s2, q2, s3, q3,
):
    mz = lax.axis_index("dir")
    mb = lax.axis_index("bl")
    z_peers = [lax.rem(mz + k, nz) for k in range(1, nz)]
    b_peers = [lax.rem(mb + k, nb) for k in range(1, nb)]

    barrier = pltpu.get_barrier_semaphore()
    for p in b_peers:
        pl.semaphore_signal(barrier, 1, device_id=(p, mz), device_id_type=MESH_ID)
    for p in z_peers:
        pl.semaphore_signal(barrier, 1, device_id=(mb, p), device_id_type=MESH_ID)

    which = which_ref[0]
    gain_start = table_ref[which]
    coher_now = rows_of(coher_ref[which].astype(jnp.float32))
    onehot_p = onehot_p_ref[...]
    onehot_q = onehot_q_ref[...]
    start_model = model_rows(split_three(gain_start), coher_now, onehot_p, onehot_q)
    residual_rows = rows_of(residual_ref[...])
    target = [residual_rows[i] + start_model[i] for i in range(8)]
    damp_value = damp_ref[0, 0]
    groups = None
    pairs = None
    per = pay.shape[1]

    def exchange(peers, src_of, buf, me, send_sems, recv_sems, device_of, r):
        sent = []
        for p in peers:
            c = pltpu.make_async_remote_copy(
                src_ref=src_of(p),
                dst_ref=buf.at[r, me],
                send_sem=send_sems.at[r, p],
                recv_sem=recv_sems.at[r, me],
                device_id=device_of(p),
                device_id_type=MESH_ID,
            )
            c.start()
            sent.append(c)
        for p in peers:
            pltpu.make_async_remote_copy(
                src_ref=buf.at[r, p],
                dst_ref=buf.at[r, p],
                send_sem=send_sems.at[r, p],
                recv_sem=recv_sems.at[r, p],
                device_id=device_of(p),
                device_id_type=MESH_ID,
            ).wait_recv()
        for c in sent:
            c.wait_send()

    def local_sums(gain_now):
        parts = split_three(gain_now)
        gain_p = rows_of(gather_cols(parts, onehot_p))
        gain_q = rows_of(gather_cols(parts, onehot_q))
        z_rows = matmul_rows(coher_now, adjoint_rows(gain_q))
        y_rows = matmul_rows(adjoint_rows(coher_now), adjoint_rows(gain_p))
        zero_row = jnp.zeros_like(target[0])
        leading = (
            matmul_rows(target, adjoint_rows(z_rows))
            + gram_rows(matmul_rows(z_rows, adjoint_rows(z_rows)))
            + [zero_row] * 4
        )
        second = (
            matmul_rows(adjoint_rows(target), adjoint_rows(y_rows))
            + gram_rows(matmul_rows(y_rows, adjoint_rows(y_rows)))
            + [zero_row] * 4
        )
        sums = scatter_cols(jnp.concatenate(leading, 0), onehot_p) + scatter_cols(
            jnp.concatenate(second, 0), onehot_q
        )
        groups = sums.shape[1] // 128
        pairs = sums.shape[0] // 2
        for g in range(groups):
            for h in range(pairs):
                slab = g * pairs + h
                pay[slab // per, slab % per] = sums[2 * h : 2 * h + 2, 128 * g : 128 * g + 128]
        return groups, pairs

    def all_reduce(r):
        exchange(b_peers, lambda p: pay.at[p], r1, mb, s1, q1, lambda p: (p, mz), r)
        own = pay[mb]
        for p in b_peers:
            own = own + r1[r, p]
        r2[r, mz] = own
        exchange(z_peers, lambda p: r2.at[r, mz], r2, mz, s2, q2, lambda p: (mb, p), r)
        total = r2[r, mz]
        for p in z_peers:
            total = total + r2[r, p]
        r3[r, mb] = total
        exchange(b_peers, lambda p: r3.at[r, mb], r3, mb, s3, q3, lambda p: (p, mz), r)

    def solve(gain_now, groups, pairs, r):
        gathered = []
        for h in range(pairs):
            for t in range(2):
                pieces = []
                for g in range(groups):
                    slab = g * pairs + h
                    pieces.append(r3[r, slab // per, slab % per, t : t + 1, :])
                gathered.append(jnp.concatenate(pieces, 1))
        gain_rows = rows_of(gain_now)
        numerator = [gathered[i] + damp_value * gain_rows[i] for i in range(8)]
        diag_a = gathered[8] + damp_value
        diag_d = gathered[9] + damp_value
        cross_r = gathered[10]
        cross_i = gathered[11]
        determinant = diag_a * diag_d - cross_r * cross_r - cross_i * cross_i
        zeros_row = jnp.zeros_like(determinant)
        inverse = [
            v / determinant
            for v in (diag_d, zeros_row, -cross_r, -cross_i, -cross_r, cross_i, diag_a, zeros_row)
        ]
        return jnp.concatenate(matmul_rows(numerator, inverse), 0)

    gain_now = gain_start
    groups, pairs = local_sums(gain_now)
    pl.semaphore_wait(barrier, (nz - 1) + (nb - 1))
    all_reduce(0)
    gain_now = solve(gain_now, groups, pairs, 0)
    for r in range(1, rounds):
        local_sums(gain_now)
        all_reduce(r)
        gain_now = solve(gain_now, groups, pairs, r)
    for d in range(table_ref.shape[0]):
        table_out[d] = jnp.where(which == d, gain_now, table_ref[d])
    final_model = model_rows(split_three(gain_now), coher_now, onehot_p, onehot_q)
    res_out[...] = jnp.concatenate([target[i] - final_model[i] for i in range(8)], 0)


def matmul_rows(left, right):
    pieces = []
    for i in (0, 1):
        for j in (0, 1):
            left_r0, left_i0 = left[4 * i], left[4 * i + 1]
            left_r1, left_i1 = left[4 * i + 2], left[4 * i + 3]
            right_r0, right_i0 = right[2 * j], right[2 * j + 1]
            right_r1, right_i1 = right[4 + 2 * j], right[4 + 2 * j + 1]
            pieces.append(
                left_r0 * right_r0 - left_i0 * right_i0 + left_r1 * right_r1 - left_i1 * right_i1
            )
            pieces.append(
                left_r0 * right_i0 + left_i0 * right_r0 + left_r1 * right_i1 + left_i1 * right_r1
            )
    return pieces


def adjoint_rows(mat):
    return [mat[0], -mat[1], mat[4], -mat[5], mat[2], -mat[3], mat[6], -mat[7]]


def gram_rows(gram):
    return [gram[0], gram[6], gram[2], gram[3]]


def damped_rounds(
    rounds, which, damp_value, gain_table, residual, coher_all, onehot_p, onehot_q, nb, nz
):
    stations = gain_table.shape[2]
    per = (16 * stations) // (nb * 2 * 128)
    vmem = pl.BlockSpec(memory_space=pltpu.VMEM)
    smem = pl.BlockSpec(memory_space=pltpu.SMEM)
    return pl.pallas_call(
        functools.partial(round_kernel, nb, nz, rounds),
        out_shape=(
            jax.ShapeDtypeStruct(gain_table.shape, gain_table.dtype),
            jax.ShapeDtypeStruct(residual.shape, residual.dtype),
        ),
        in_specs=[smem, smem] + [vmem] * 5,
        out_specs=(vmem, vmem),
        scratch_shapes=[
            pltpu.VMEM((nb, per, 2, 128), jnp.float32),
            pltpu.VMEM((rounds, nb, per, 2, 128), jnp.float32),
            pltpu.VMEM((rounds, nz, per, 2, 128), jnp.float32),
            pltpu.VMEM((rounds, nb, per, 2, 128), jnp.float32),
            pltpu.SemaphoreType.DMA((rounds, nb)),
            pltpu.SemaphoreType.DMA((rounds, nb)),
            pltpu.SemaphoreType.DMA((rounds, nz)),
            pltpu.SemaphoreType.DMA((rounds, nz)),
            pltpu.SemaphoreType.DMA((rounds, nb)),
            pltpu.SemaphoreType.DMA((rounds, nb)),
        ],
        compiler_params=pltpu.CompilerParams(collective_id=2 * rounds, has_side_effects=True),
    )(
        which.reshape(1), damp_value.reshape(1, 1), gain_table, residual, coher_all, onehot_p,
        onehot_q,
    )


def prologue_kernel(nb, nz, coh_ref, gain_ref, coh_out, gain_out, coh_buf, gain_buf, s1, q1, s2, q2):
    mz = lax.axis_index("dir")
    mb = lax.axis_index("bl")
    z_peers = [lax.rem(mz + k, nz) for k in range(1, nz)]
    b_peers = [lax.rem(mb + k, nb) for k in range(1, nb)]

    barrier = pltpu.get_barrier_semaphore()
    for p in b_peers:
        pl.semaphore_signal(barrier, 1, device_id=(p, mz), device_id_type=MESH_ID)
    for p in z_peers:
        pl.semaphore_signal(barrier, 1, device_id=(mb, p), device_id_type=MESH_ID)
    pl.semaphore_wait(barrier, (nz - 1) + (nb - 1))

    sent = []
    for p in z_peers:
        c = pltpu.make_async_remote_copy(
            src_ref=coh_ref.at[p],
            dst_ref=coh_buf.at[mz],
            send_sem=s1.at[p],
            recv_sem=q1.at[mz],
            device_id=(mb, p),
            device_id_type=MESH_ID,
        )
        c.start()
        sent.append(c)
    for p in b_peers:
        c = pltpu.make_async_remote_copy(
            src_ref=gain_ref,
            dst_ref=gain_buf.at[mb],
            send_sem=s2.at[p],
            recv_sem=q2.at[mb],
            device_id=(p, mz),
            device_id_type=MESH_ID,
        )
        c.start()
        sent.append(c)
    coh_buf[mz] = coh_ref[mz]
    gain_buf[mb] = gain_ref[...]
    for p in z_peers:
        pltpu.make_async_remote_copy(
            src_ref=coh_buf.at[p],
            dst_ref=coh_buf.at[p],
            send_sem=s1.at[p],
            recv_sem=q1.at[p],
            device_id=(mb, p),
            device_id_type=MESH_ID,
        ).wait_recv()
    for p in b_peers:
        pltpu.make_async_remote_copy(
            src_ref=gain_buf.at[p],
            dst_ref=gain_buf.at[p],
            send_sem=s2.at[p],
            recv_sem=q2.at[p],
            device_id=(p, mz),
            device_id_type=MESH_ID,
        ).wait_recv()
    for c in sent:
        c.wait_send()
    coh_out[...] = coh_buf[...]
    gain_out[...] = gain_buf[...]


def exchange_inputs(coh_by_channel, gain_block, nb, nz):
    vmem = pl.BlockSpec(memory_space=pltpu.VMEM)
    coh_shape = (nz,) + coh_by_channel.shape[1:]
    gain_shape = (nb,) + gain_block.shape
    return pl.pallas_call(
        functools.partial(prologue_kernel, nb, nz),
        out_shape=(
            jax.ShapeDtypeStruct(coh_shape, coh_by_channel.dtype),
            jax.ShapeDtypeStruct(gain_shape, gain_block.dtype),
        ),
        in_specs=[vmem, vmem],
        out_specs=(vmem, vmem),
        scratch_shapes=[
            pltpu.VMEM(coh_shape, coh_by_channel.dtype),
            pltpu.VMEM(gain_shape, gain_block.dtype),
            pltpu.SemaphoreType.DMA((nz,)),
            pltpu.SemaphoreType.DMA((nz,)),
            pltpu.SemaphoreType.DMA((nb,)),
            pltpu.SemaphoreType.DMA((nb,)),
        ],
        compiler_params=pltpu.CompilerParams(collective_id=1, has_side_effects=True),
    )(coh_by_channel, gain_block)


def on_device(visibilities, coherencies, gain_offsets, stations, solve_order, counts, damping):
    identity = jnp.zeros((8,), jnp.float32).at[0].set(1.0).at[6].set(1.0)
    groups = lax.axis_size("bl")
    nz = lax.axis_size("dir")
    owned, _, channels_all, width = coherencies.shape
    by_channel = jnp.transpose(coherencies, (2, 0, 1, 3)).reshape(channels_all, owned * 8, width)
    coh_recv, gain_recv = exchange_inputs(
        by_channel, gain_offsets.reshape(-1, 128), groups, nz
    )
    direction_total = gain_offsets.shape[0]
    offsets = jnp.transpose(
        gain_recv.reshape((groups,) + gain_offsets.shape), (1, 2, 0, 3)
    ).reshape(direction_total, 8, groups * gain_offsets.shape[2])
    start = offsets + identity[None, :, None]
    coher_all = coh_recv.reshape(nz * owned, 8, 1, width)
    total_channels = coherencies.shape[2]
    station_count = start.shape[2]
    damping_factor = visibilities.shape[2] * groups * total_channels / station_count
    start_by_entry = jnp.transpose(start, (1, 0, 2))
    gain_p = jnp.take(start_by_entry, stations[0], axis=2)[:, :, None, :]
    gain_q = jnp.take(start_by_entry, stations[1], axis=2)[:, :, None, :]
    coher_f32 = jnp.transpose(coher_all, (1, 0, 2, 3)).astype(jnp.float32)
    first_model = jnp.sum(apply_gains(gain_p, coher_f32, gain_q), axis=1)
    first_residual = visibilities - first_model

    station_ids = lax.broadcasted_iota(jnp.int32, (station_count, stations.shape[1]), 0)
    onehot_p = (station_ids == stations[0][None, :]).astype(jnp.bfloat16)
    onehot_q = (station_ids == stations[1][None, :]).astype(jnp.bfloat16)

    def direction_model(gain_now, coher_now):
        gain_p = jnp.take(gain_now, stations[0], axis=1)[:, None, :]
        gain_q = jnp.take(gain_now, stations[1], axis=1)[:, None, :]
        return apply_gains(gain_p, coher_now, gain_q)

    coher_rows = coher_all.reshape(coher_all.shape[0], 8, coher_all.shape[3])

    def sweep(step_index, state):
        gain_table, residual = state
        which = solve_order[step_index]
        damp_value = damping[which].astype(jnp.float32) * damping_factor

        def run(rounds):
            def branch(operands):
                if rounds == 0:
                    return (gain_table, residual)
                return damped_rounds(
                    rounds, which, damp_value, gain_table, residual, coher_rows,
                    onehot_p, onehot_q, groups, nz,
                )

            return branch

        return lax.cond(counts[which] >= LM_ITERS, run(LM_ITERS), run(1), None)

    gain_table, residual_rows = lax.fori_loop(
        0, SOLVED, sweep, (start, first_residual[:, 0, :])
    )
    residual = residual_rows[:, None, :]
    own_width = station_count // groups
    gains = lax.dynamic_slice_in_dim(gain_table, lax.axis_index("bl") * own_width, own_width, 2)
    return (gains, residual)


def solution(mesh):
    return jax.shard_map(
        on_device,
        mesh=mesh,
        in_specs=(
            P(None, "dir", "bl"),
            P("dir", None, None, "bl"),
            P(None, None, "bl"),
            P(None, "bl"),
            P(),
            P(),
            P(),
        ),
        out_specs=(P(None, None, "bl"), P(None, "dir", "bl")),
        check_vma=False,
    )
```
